32 devices in a mesh: dp: 16 (over z, y, core), seq: 2 (over x).
Axes of the slice: x: 2, y: 2, z: 4, core: 2. Of those that a mesh axis runs over, the one named last changes fastest.
Arguments:
- pre_act: bfloat16 [16, 512, 768], P('dp', 'seq'), may hold values from -6 to 6
- trunk_grad: bfloat16 [16, 256, 768], P('dp', None, 'seq'), may hold values from -6 to 6
- conv_weight: bfloat16 [5, 768, 768], P(None, 'dp'), may hold values from -0.09375 to 0.09375
- pair_weight: bfloat16 [768, 768], replicated, may hold values from -0.21875 to 0.21875
- donor_slots: int32 [16, 2, 2, 128], P('dp', 'seq'), may hold values from 0 to 255
- accept_slots: int32 [16, 2, 2, 128], P('dp', 'seq'), may hold values from 0 to 255
- junction_grad: float32 [16, 2, 2, 128], P('dp', 'seq'), may hold values from -6 to 6
- pair_counts: int32 [16, 2, 2], P('dp'), may hold values from 0 to 128, as said below
Outputs:
- input_grad: bfloat16 [16, 512, 768], P('dp', 'seq')
- pair_grad: float32 [768, 768], replicated
The draws below stay inside these ranges and needn't reach their ends.
Inputs may be any that keep to these rules, and one draw needn't show every extreme that they name: pair_counts is at most 128; in every sample some acceptor slab has 128 live slots from every donor slab.
All inputs are finite; a program needn't handle non-finite values.
Results may differ from the reference program's by a relative error of at most 0.0061.
Values may be sent and summed in bfloat16 or wider, within the bound.
A program may use at most 64 MiB of HBM per device.

```python
import math
import jax
import jax.numpy as jnp
from jax import lax

CHANNELS = 768
KERNEL = 5
SLOTS = 128
SLAB = 256
SAMPLES = 16
SEQ_LEN = 512
TOKENS = 256
JUNCTION_SLOTS = 8192
N_SEQ = 2


def draw_pair_counts(key, part):
    first, second, third = jax.random.split(jax.random.fold_in(key, 11), 3)
    left = jax.random.randint(first, (SAMPLES, N_SEQ, N_SEQ), 0, SLOTS + 1)
    right = jax.random.randint(second, (SAMPLES, N_SEQ, N_SEQ), 0, SLOTS + 1)
    counts = jnp.maximum(left, right)
    full_col = jax.random.randint(third, (SAMPLES,), 0, N_SEQ)
    column = jnp.arange(N_SEQ, dtype=jnp.int32)[None, None, :]
    counts = jnp.where(column == full_col[:, None, None], SLOTS, counts)
    return counts.astype(jnp.int32)


def plant(result, key, low, largest):
    extent = result.shape
    spot = [jax.random.randint(jax.random.fold_in(key, axis), (), 0, extent[axis]) for axis in range(len(extent))]
    result = result.at[tuple(spot)].set(low)
    longest = extent.index(max(extent))
    spot[longest] = (spot[longest] + 1) % extent[longest]
    return result.at[tuple(spot)].set(largest)


def block_scale(key, shape, shards, least, largest):
    loudness = 1.0
    for position, shards_of in shards:
        steps = jax.random.uniform(jax.random.fold_in(jax.random.fold_in(key, 6), position), (shards_of,), jnp.float32, least / len(shards), largest / len(shards))
        loudness = loudness * jnp.repeat(jnp.exp(steps), shape[position] // shards_of).reshape((-1,) + (1,) * (len(shape) - 1 - position))
    return loudness


def scatter_about(key, dims, deviation, reach, cuts=(), kind=jnp.bfloat16):
    drawn = jax.random.normal(key, dims, jnp.float32) * deviation
    if len(cuts) > 0:
        drawn = block_scale(key, dims, cuts, -0.22, 0.18) * drawn
    return jnp.clip(drawn, min=-reach, max=reach).astype(kind)


def setup_inputs(seed: int = 0) -> dict:
    splits = jax.random.split(jax.random.key(seed), 9)
    pre_act = scatter_about(splits[0], (SAMPLES, SEQ_LEN, CHANNELS), 1.0, 6.0, ((0, 16), (1, 2)))
    trunk_grad = scatter_about(splits[1], (SAMPLES, TOKENS, CHANNELS), 1.0, 6.0, ((0, 16), (2, 2)))
    conv_weight = scatter_about(splits[2], (KERNEL, CHANNELS, CHANNELS), (KERNEL * CHANNELS) ** -0.5, 0.09375, ((1, 16),))
    pair_weight = scatter_about(splits[3], (CHANNELS, CHANNELS), CHANNELS ** -0.5, 0.21875)
    donor_slots = plant(jax.random.randint(splits[4], (SAMPLES, N_SEQ, N_SEQ, SLOTS), 0, SLAB), jax.random.fold_in(splits[4], 1), 0, SLAB - 1).astype(jnp.int32)
    accept_slots = plant(jax.random.randint(splits[5], (SAMPLES, N_SEQ, N_SEQ, SLOTS), 0, SLAB), jax.random.fold_in(splits[5], 1), 0, SLAB - 1).astype(jnp.int32)
    junction_grad = scatter_about(splits[6], (SAMPLES, N_SEQ, N_SEQ, SLOTS), 1.0, 6.0, ((0, 16), (1, 2)), jnp.float32)
    pair_counts = draw_pair_counts(jax.random.fold_in(splits[8], 71), 0)
    return dict(pre_act=pre_act, trunk_grad=trunk_grad, conv_weight=conv_weight, pair_weight=pair_weight, donor_slots=donor_slots, accept_slots=accept_slots, junction_grad=junction_grad, pair_counts=pair_counts)


def gelu_parts(values):
    normal_cdf = 0.5 * (1.0 + jax.scipy.special.erf(values / math.sqrt(2.0)))
    density = jnp.exp(-0.5 * values * values) / math.sqrt(2.0 * math.pi)
    return (values * normal_cdf, normal_cdf + values * density)

def per_sample(carry, inputs):
    pre, grad_tok, donors, accepts, weights_in, counts, conv_weight, pair_weight = inputs
    act_f, slope = gelu_parts(pre.astype(jnp.float32))
    act = act_f.astype(jnp.bfloat16)
    pooled = jnp.repeat(grad_tok.astype(jnp.float32) * 0.5, 2, axis=0)
    offsets = jnp.arange(N_SEQ, dtype=jnp.int32) * SLAB
    donor_glob = (jnp.transpose(donors, (1, 0, 2)) + offsets[None, :, None]).reshape(-1).astype(jnp.int32)
    accept_glob = (accepts + offsets[:, None, None]).reshape(-1).astype(jnp.int32)
    live = jnp.arange(SLOTS, dtype=jnp.int32)[None, None, :] < jnp.transpose(counts)[:, :, None]
    slot_w = jnp.where(live, weights_in, 0.0).reshape(-1)
    donor_rows = act[donor_glob]
    accept_rows = act[accept_glob]
    weighted = (slot_w[:, None] * accept_rows.astype(jnp.float32)).astype(jnp.bfloat16)
    accept_term = jnp.dot(donor_rows, pair_weight, preferred_element_type=jnp.float32) * slot_w[:, None]
    donor_term = lax.dot_general(weighted, pair_weight, (((1,), (1,)), ((), ())), preferred_element_type=jnp.float32).astype(jnp.bfloat16)
    pair_part = lax.dot_general(donor_rows, weighted, (((0,), (0,)), ((), ())), preferred_element_type=jnp.float32)
    act_grad = pooled.at[accept_glob].add(accept_term).at[donor_glob].add(donor_term.astype(jnp.float32))
    conv_grad = (act_grad * slope).astype(jnp.bfloat16)
    half = KERNEL // 2
    padded = jnp.pad(conv_grad, ((half, half), (0, 0)))
    total = jnp.zeros((SEQ_LEN, CHANNELS), jnp.float32)
    for tap in range(KERNEL):
        window = padded[2 * half - tap:2 * half - tap + SEQ_LEN]
        total = total + lax.dot_general(window, conv_weight[tap], (((1,), (1,)), ((), ())), preferred_element_type=jnp.float32)
    return (carry + pair_part, total.astype(jnp.bfloat16))

def reference(pre_act, trunk_grad, conv_weight, pair_weight, donor_slots, accept_slots, junction_grad, pair_counts):

    def step(carry, inputs):
        pre, grad_tok, donors, accepts, weights_in, counts = inputs
        return per_sample(carry, (pre, grad_tok, donors, accepts, weights_in, counts, conv_weight, pair_weight))
    start = jnp.zeros((CHANNELS, CHANNELS), jnp.float32)
    pair_sum, input_grad = lax.scan(step, start, (pre_act, trunk_grad, donor_slots, accept_slots, junction_grad, pair_counts))
    pair_grad = pair_sum * (1.0 / math.sqrt(JUNCTION_SLOTS))
    return (input_grad, pair_grad)
```

```python
import math

import jax
import jax.numpy as jnp
from jax import lax
from jax.experimental import pallas as pl
from jax.experimental.pallas import tpu as pltpu
from jax.sharding import PartitionSpec as P


def with_halo(x, sides, width):
    for axis, dim in sides:
        size, length = (lax.axis_size(axis), x.shape[dim])
        up = [(i, (i + 1) % size) for i in range(size - 1)]
        down = [(j, i) for i, j in up]
        last = lax.slice_in_dim(x, length - width, length, axis=dim)
        first = lax.slice_in_dim(x, 0, width, axis=dim)
        before = lax.ppermute(last, axis, up)
        after = lax.ppermute(first, axis, down)
        x = jnp.concatenate([before, x, after], axis=dim)
    return x


def gelu_parts(values):
    normal_cdf = 0.5 * (1.0 + jax.scipy.special.erf(values / math.sqrt(2.0)))
    density = jnp.exp(-0.5 * values * values) / math.sqrt(2.0 * math.pi)
    return (values * normal_cdf, normal_cdf + values * density)


def per_device_general(
    pre_act,
    trunk_grad,
    conv_weight,
    pair_weight,
    donor_slots,
    accept_slots,
    junction_grad,
    pair_counts,
):
    seq_count = lax.axis_size("seq")
    my_slab = lax.axis_index("seq")
    slab_len = pre_act.shape[1]
    channels = pre_act.shape[2]
    slot_count = donor_slots.shape[3]
    kernel = conv_weight.shape[0]
    half = kernel // 2
    act_f, slope = gelu_parts(pre_act[0].astype(jnp.float32))
    act = act_f.astype(jnp.bfloat16)
    arrived = lax.all_to_all(trunk_grad, "seq", split_axis=1, concat_axis=2, tiled=True)
    pooled = jnp.repeat(arrived[0].astype(jnp.float32) * 0.5, 2, axis=0)
    send_index = donor_slots[0, 0].reshape(-1)
    outgoing = act[send_index].reshape(seq_count, slot_count, channels)
    incoming = lax.all_to_all(outgoing, "seq", split_axis=0, concat_axis=0, tiled=True)
    donor_rows = incoming.reshape(-1, channels)
    accept_index = accept_slots[0, 0].reshape(-1)
    counts_in = lax.dynamic_index_in_dim(pair_counts[0], my_slab, axis=1, keepdims=False)
    live = jnp.arange(slot_count, dtype=jnp.int32)[None, :] < counts_in[:, None]
    slot_w = jnp.where(live, junction_grad[0, 0], 0.0).reshape(-1)
    accept_rows = act[accept_index]
    weighted = (slot_w[:, None] * accept_rows.astype(jnp.float32)).astype(jnp.bfloat16)
    accept_term = (
        jnp.dot(donor_rows, pair_weight, preferred_element_type=jnp.float32) * slot_w[:, None]
    )
    donor_term = lax.dot_general(
        weighted, pair_weight, (((1,), (1,)), ((), ())), preferred_element_type=jnp.float32
    ).astype(jnp.bfloat16)
    pair_part = lax.dot_general(
        donor_rows, weighted, (((0,), (0,)), ((), ())), preferred_element_type=jnp.float32
    )
    returned = lax.all_to_all(
        donor_term.reshape(seq_count, slot_count, channels),
        "seq",
        split_axis=0,
        concat_axis=0,
        tiled=True,
    )
    act_grad = (
        pooled.at[accept_index]
        .add(accept_term)
        .at[send_index]
        .add(returned.reshape(-1, channels).astype(jnp.float32))
    )
    conv_grad = (act_grad * slope).astype(jnp.bfloat16)
    padded = with_halo(conv_grad[None], (("seq", 1),), half)[0]
    piece = lax.all_gather(conv_weight, "dp", axis=1, tiled=True)
    total = jnp.zeros((slab_len, piece.shape[1]), jnp.float32)
    for tap in range(kernel):
        window = padded[2 * half - tap : 2 * half - tap + slab_len]
        total = total + lax.dot_general(
            window, piece[tap], (((1,), (1,)), ((), ())), preferred_element_type=jnp.float32
        )
    input_grad = total.astype(jnp.bfloat16)
    pair_sum = lax.psum(pair_part, ("dp", "seq"))
    scale = 1.0 / math.sqrt(lax.axis_size("dp") * seq_count * seq_count * slot_count)
    return (input_grad[None], pair_sum * scale)


MESH = pl.DeviceIdType.MESH
NZ, NY, NC = 4, 2, 2
ROWS_T = (((0,), (0,)), ((), ()))
COLS_T = (((1,), (1,)), ((), ()))


def dot(a, b):
    return jnp.dot(a, b, preferred_element_type=jnp.float32)


def kernel(
    pre_ref, trunk_ref, w_ref, p_ref, ds_ref, as_ref, jg_ref, pc_ref,
    out_ref, pair_ref,
    act_s, slope_s, wbuf, trunk_in, dsend, drecv, tsend, trecv, drows, weighted_s, zbuf,
    pad_s, halo_send, halo_recv, part_s, c_send, c_recv, x_send, x_recv, own_s, r_send, r_recv,
    final,
    wz_s, wz_r, wy_s, wy_r, wc_s, wc_r, loc_sem, xs_s, xs_r, ar_s, ar_r, rs_s, rs_r, ag_s, ag_r,
):
    dp = lax.axis_index("dp")
    x = lax.axis_index("seq")
    c = dp % 2
    y = (dp // 2) % 2
    z = dp // 4
    me8 = dp // 2
    ox = 1 - x
    oc = 1 - c
    chan = pre_ref.shape[2]
    slots = ds_ref.shape[-1]
    shard = w_ref.shape[1]
    hc = chan // 2
    slab = pre_ref.shape[1]
    tok = slab // 2

    def dev(zz, yy, cc):
        return (zz * NY + yy) * NC + cc

    def peer8(k):
        return lax.rem(me8 + k, 8)

    barrier = pltpu.get_barrier_semaphore()
    for k in range(1, 8):
        pl.semaphore_signal(barrier, inc=1, device_id=(peer8(k) * 2 + c, x), device_id_type=MESH)
    pl.semaphore_signal(barrier, inc=1, device_id=(me8 * 2 + oc, x), device_id_type=MESH)
    pl.semaphore_signal(barrier, inc=1, device_id=(dp, ox), device_id_type=MESH)
    pl.semaphore_wait(barrier, 9)

    def remote(src, dst, ss, rs, target):
        return pltpu.make_async_remote_copy(
            src_ref=src, dst_ref=dst, send_sem=ss, recv_sem=rs,
            device_id=target, device_id_type=MESH,
        )

    def wblock(index):
        return wbuf.at[:, pl.ds(pl.multiple_of(index * shard, 16), shard), :]

    xdev = (dp, ox)
    cdev = (me8 * 2 + oc, x)
    ydev = (dev(z, 1 - y, c), x)

    trunk_copy = remote(
        trunk_ref.at[0, pl.ds(pl.multiple_of(ox * tok, 16), tok), :], trunk_in,
        xs_s.at[0], xs_r.at[0], xdev)
    trunk_copy.start()
    wz = [None]
    for k in range(1, NZ):
        cp = remote(w_ref, wblock(dp), wz_s.at[k], wz_r.at[k],
                    (dev(lax.rem(z + k, NZ), y, c), x))
        cp.start()
        wz.append(cp)
    wy = [remote(w_ref, wblock(dp), wy_s.at[0], wy_r.at[0], ydev)]
    wy[0].start()
    wcore = {}
    wcore[0, 0] = remote(w_ref, wblock(dp), wc_s.at[0], wc_r.at[0], cdev)
    wcore[0, 0].start()
    own_w = pltpu.make_async_copy(w_ref, wblock(dp), loc_sem)
    own_w.start()

    def pass_z(k):
        wz[k].wait_recv()
        block = wblock(dev(lax.rem(z + NZ - k, NZ), y, c))
        cp = remote(block, block, wy_s.at[k], wy_r.at[k], ydev)
        cp.start()
        wy.append(cp)
        cp = remote(block, block, wc_s.at[k], wc_r.at[k], cdev)
        cp.start()
        wcore[0, k] = cp

    def pass_y(k):
        wy[k].wait_recv()
        block = wblock(dev(lax.rem(z + NZ - k, NZ), 1 - y, c))
        cp = remote(block, block, wc_s.at[4 + k], wc_r.at[4 + k], cdev)
        cp.start()
        wcore[1, k] = cp

    act_f, slope = gelu_parts(pre_ref[0].astype(jnp.float32))
    act_s[...] = act_f.astype(jnp.bfloat16)
    slope_s[...] = slope

    first = x == 0

    def loc_oth(rows):
        a, b = rows[0:1], rows[1:2]
        return jnp.where(first, a, b), jnp.where(first, b, a)

    d_loc, d_oth = loc_oth(ds_ref[0, 0])
    a_loc, a_oth = loc_oth(as_ref[0, 0])
    counts = pc_ref[0]
    cnt = jnp.where(first, counts[:, 0:1], counts[:, 1:2])
    live = lax.broadcasted_iota(jnp.int32, (2, slots), 1) < cnt
    w_loc, w_oth = loc_oth(jnp.where(live, jg_ref[0, 0], 0.0))

    position = lax.broadcasted_iota(jnp.int32, (slab, slots), 0)

    def onehot(row):
        return jnp.where(position == row, 1.0, 0.0)

    td_oth, td_loc, ta_oth, ta_loc = [onehot(r) for r in (d_oth, d_loc, a_oth, a_loc)]

    def flip(m):
        return jnp.transpose(m).astype(jnp.bfloat16)

    def column(row):
        return jnp.transpose(jnp.broadcast_to(row, (slots, slots)))[:, 0:1]

    dsend[...] = dot(flip(td_oth), act_s[...]).astype(jnp.bfloat16)
    d_copy = remote(dsend, drecv, xs_s.at[1], xs_r.at[1], xdev)
    d_copy.start()

    wc_oth, wc_loc = column(w_oth), column(w_loc)
    rows = dot(flip(ta_oth), act_s[...])
    weighted_s[0:slots, :] = (wc_oth * rows).astype(jnp.bfloat16)
    tsend[...] = lax.dot_general(
        weighted_s[0:slots, :], p_ref[...], COLS_T, preferred_element_type=jnp.float32
    ).astype(jnp.bfloat16)
    t_copy = remote(tsend, trecv, xs_s.at[2], xs_r.at[2], xdev)
    t_copy.start()

    rows = dot(flip(ta_loc), act_s[...])
    weighted_s[slots:, :] = (wc_loc * rows).astype(jnp.bfloat16)
    zbuf[3 * slots : 4 * slots, :] = lax.dot_general(
        weighted_s[slots:, :], p_ref[...], COLS_T, preferred_element_type=jnp.float32
    ).astype(jnp.bfloat16)
    drows[slots:, :] = dot(flip(td_loc), act_s[...]).astype(jnp.bfloat16)
    zbuf[slots : 2 * slots, :] = (
        dot(drows[slots:, :], p_ref[...]) * wc_loc
    ).astype(jnp.bfloat16)

    d_copy.wait_recv()
    drows[0:slots, :] = drecv[...]
    part_s[...] = lax.dot_general(
        drows[...], weighted_s[...], ROWS_T, preferred_element_type=jnp.float32)
    c_send[...] = part_s[pl.ds(pl.multiple_of(oc * hc, 8), hc), :].astype(jnp.bfloat16)
    c_copy = remote(c_send, c_recv, ar_s.at[0], ar_r.at[0], cdev)
    c_copy.start()
    zbuf[0:slots, :] = (dot(drows[0:slots, :], p_ref[...]) * wc_oth).astype(jnp.bfloat16)

    trunk_copy.wait_recv()
    mine = trunk_ref[0, pl.ds(pl.multiple_of(x * tok, 16), tok), :]
    zbuf[4 * slots :, 0:hc] = jnp.where(first, mine, trunk_in[...])
    zbuf[4 * slots :, hc:] = jnp.where(first, trunk_in[...], mine)
    t_copy.wait_recv()
    zbuf[2 * slots : 3 * slots, :] = trecv[...]
    spread = jnp.where(
        lax.broadcasted_iota(jnp.int32, (slab, tok), 0) // 2
        == lax.broadcasted_iota(jnp.int32, (slab, tok), 1), 0.5, 0.0)
    scatter = jnp.concatenate([ta_oth, ta_loc, td_oth, td_loc, spread], axis=1).astype(jnp.bfloat16)
    grad = (dot(scatter, zbuf[...]) * slope_s[...]).astype(jnp.bfloat16).astype(jnp.float32)
    pad_s[8 : 8 + slab, :] = grad
    halo_send[0:8, :] = grad[0:8]
    halo_send[8:16, :] = grad[slab - 8 : slab]
    h_copy = remote(halo_send, halo_recv, xs_s.at[3], xs_r.at[3], xdev)
    h_copy.start()

    c_copy.wait_recv()
    half = part_s[pl.ds(pl.multiple_of(c * hc, 8), hc), :] + c_recv[...].astype(jnp.float32)
    left, right = half[:, 0:hc], half[:, hc:]
    own_s[...] = jnp.where(first, left, right)
    x_send[...] = jnp.where(first, right, left).astype(jnp.bfloat16)
    x_copy = remote(x_send, x_recv, ar_s.at[1], ar_r.at[1], xdev)
    x_copy.start()

    pass_z(1)

    h_copy.wait_recv()
    nothing = jnp.zeros((8, chan), jnp.float32)
    pad_s[0:8, :] = jnp.where(first, nothing, halo_recv[8:16, :])
    pad_s[8 + slab :, :] = jnp.where(first, halo_recv[0:8, :], nothing)

    x_copy.wait_recv()
    own_s[...] = own_s[...] + x_recv[...].astype(jnp.float32)
    r_send[...] = own_s[...].astype(jnp.bfloat16)
    piece = hc // 8
    rs = []
    for k in range(1, 8):
        to = peer8(k)
        cp = remote(r_send.at[pl.ds(pl.multiple_of(to * piece, 16), piece), :], r_recv.at[k - 1],
                    rs_s.at[k - 1], rs_r.at[k - 1], (to * 2 + c, x))
        cp.start()
        rs.append(cp)

    pass_z(2)
    pass_z(3)
    for cp in rs:
        cp.wait_recv()
    total = own_s[pl.ds(pl.multiple_of(me8 * piece, 8), piece), :]
    for k in range(7):
        total = total + r_recv[k].astype(jnp.float32)

    def fblock(cc, xx, start, size):
        return final.at[pl.ds(pl.multiple_of(cc * hc + start, 16), size),
                        pl.ds(pl.multiple_of(xx * hc, 128), hc)]

    r_done = r_send
    for cp in rs:
        cp.wait_send()
    r_done[0:piece, :] = total.astype(jnp.bfloat16)
    mine_to = pltpu.make_async_copy(
        r_done.at[0:piece, :], fblock(c, x, me8 * piece, piece), ar_s.at[5])
    mine_to.start()
    ag = []
    for k in range(1, 8):
        cp = remote(r_done.at[0:piece, :], fblock(c, x, me8 * piece, piece),
                    ag_s.at[k - 1], ag_r.at[k - 1], (peer8(k) * 2 + c, x))
        cp.start()
        ag.append(cp)

    pass_y(0)
    pass_y(1)
    mine_to.wait()
    for cp in ag:
        cp.wait_recv()
    quarter = fblock(c, x, 0, hc)
    xq = remote(quarter, quarter, ar_s.at[2], ar_r.at[2], xdev)
    xq.start()
    cq = remote(quarter, quarter, ar_s.at[3], ar_r.at[3], cdev)
    cq.start()
    pass_y(2)
    pass_y(3)
    xq.wait_recv()
    other = fblock(c, ox, 0, hc)
    cq2 = remote(other, other, ar_s.at[4], ar_r.at[4], cdev)
    cq2.start()

    own_w.wait()
    for cp in wcore.values():
        cp.wait_recv()
    kernel_w = w_ref.shape[0]
    shift = kernel_w // 2
    acc = None
    for tap in range(kernel_w):
        window = pad_s[8 + shift - tap : 8 + shift - tap + slab, :].astype(jnp.bfloat16)
        term = lax.dot_general(window, wbuf[tap], COLS_T, preferred_element_type=jnp.float32)
        acc = term if acc is None else acc + term
    out_ref[0] = acc.astype(jnp.bfloat16)

    cq.wait_recv()
    cq2.wait_recv()
    scale = 1.0 / math.sqrt(NZ * NY * NC * 2 * 2 * slots)
    pair_ref[...] = final[...].astype(jnp.float32) * scale
    for cp in wz[1:] + wy + list(wcore.values()) + [trunk_copy, d_copy, t_copy, h_copy, c_copy, x_copy, xq, cq, cq2] + ag:
        cp.wait_send()


def per_device_kernel(pre_act, trunk_grad, conv_weight, pair_weight, donor_slots, accept_slots, junction_grad, pair_counts):
    slab, chan = pre_act.shape[1:]
    slots = donor_slots.shape[3]
    hc = chan // 2
    bf, f32 = jnp.bfloat16, jnp.float32
    V = pltpu.VMEM
    D = pltpu.SemaphoreType.DMA
    scratch = [
        V((slab, chan), bf), V((slab, chan), f32), V((conv_weight.shape[0], chan, chan), bf),
        V((slab // 2, hc), bf), V((slots, chan), bf), V((slots, chan), bf),
        V((slots, chan), bf), V((slots, chan), bf), V((2 * slots, chan), bf),
        V((2 * slots, chan), bf), V((4 * slots + slab // 2, chan), bf),
        V((slab + 16, chan), f32), V((16, chan), f32), V((16, chan), f32),
        V((chan, chan), f32), V((hc, chan), bf), V((hc, chan), bf), V((hc, hc), bf), V((hc, hc), bf),
        V((hc, hc), f32), V((hc, hc), bf), V((7, hc // 8, hc), bf), V((chan, chan), bf),
        D((4,)), D((4,)), D((4,)), D((4,)), D((8,)), D((8,)), D, D((4,)), D((4,)),
        D((6,)), D((6,)), D((7,)), D((7,)), D((7,)), D((7,)),
    ]
    return pl.pallas_call(
        kernel,
        out_shape=(jax.ShapeDtypeStruct(pre_act.shape, bf), jax.ShapeDtypeStruct((chan, chan), f32)),
        in_specs=[pl.BlockSpec(memory_space=pltpu.VMEM)] * 8,
        out_specs=[pl.BlockSpec(memory_space=pltpu.VMEM)] * 2,
        scratch_shapes=scratch,
        compiler_params=pltpu.CompilerParams(
            collective_id=0, has_side_effects=True, vmem_limit_bytes=48 << 20),
    )(pre_act, trunk_grad, conv_weight, pair_weight, donor_slots, accept_slots, junction_grad, pair_counts)


def solution(mesh):
    in_specs = (
        P("dp", "seq", None),
        P("dp", None, "seq"),
        P(None, "dp", None),
        P(),
        P("dp", "seq", None, None),
        P("dp", "seq", None, None),
        P("dp", "seq", None, None),
        P("dp", None, None),
    )
    out_specs = (P("dp", "seq", None), P())
    fits = mesh.shape["dp"] == NZ * NY * NC and mesh.shape["seq"] == 2
    return jax.shard_map(
        per_device_kernel if fits else per_device_general, mesh=mesh, in_specs=in_specs, out_specs=out_specs, check_vma=False
    )
```

```python
import math

import jax
import jax.numpy as jnp
from jax import lax
from jax.experimental import pallas as pl
from jax.experimental.pallas import tpu as pltpu
from jax.sharding import PartitionSpec as P


def with_halo(x, sides, width):
    for axis, dim in sides:
        size, length = (lax.axis_size(axis), x.shape[dim])
        up = [(i, (i + 1) % size) for i in range(size - 1)]
        down = [(j, i) for i, j in up]
        last = lax.slice_in_dim(x, length - width, length, axis=dim)
        first = lax.slice_in_dim(x, 0, width, axis=dim)
        before = lax.ppermute(last, axis, up)
        after = lax.ppermute(first, axis, down)
        x = jnp.concatenate([before, x, after], axis=dim)
    return x


def gelu_parts(values):
    normal_cdf = 0.5 * (1.0 + jax.scipy.special.erf(values / math.sqrt(2.0)))
    density = jnp.exp(-0.5 * values * values) / math.sqrt(2.0 * math.pi)
    return (values * normal_cdf, normal_cdf + values * density)


def per_device_general(
    pre_act,
    trunk_grad,
    conv_weight,
    pair_weight,
    donor_slots,
    accept_slots,
    junction_grad,
    pair_counts,
):
    seq_count = lax.axis_size("seq")
    my_slab = lax.axis_index("seq")
    slab_len = pre_act.shape[1]
    channels = pre_act.shape[2]
    slot_count = donor_slots.shape[3]
    kernel = conv_weight.shape[0]
    half = kernel // 2
    act_f, slope = gelu_parts(pre_act[0].astype(jnp.float32))
    act = act_f.astype(jnp.bfloat16)
    arrived = lax.all_to_all(trunk_grad, "seq", split_axis=1, concat_axis=2, tiled=True)
    pooled = jnp.repeat(arrived[0].astype(jnp.float32) * 0.5, 2, axis=0)
    send_index = donor_slots[0, 0].reshape(-1)
    outgoing = act[send_index].reshape(seq_count, slot_count, channels)
    incoming = lax.all_to_all(outgoing, "seq", split_axis=0, concat_axis=0, tiled=True)
    donor_rows = incoming.reshape(-1, channels)
    accept_index = accept_slots[0, 0].reshape(-1)
    counts_in = lax.dynamic_index_in_dim(pair_counts[0], my_slab, axis=1, keepdims=False)
    live = jnp.arange(slot_count, dtype=jnp.int32)[None, :] < counts_in[:, None]
    slot_w = jnp.where(live, junction_grad[0, 0], 0.0).reshape(-1)
    accept_rows = act[accept_index]
    weighted = (slot_w[:, None] * accept_rows.astype(jnp.float32)).astype(jnp.bfloat16)
    accept_term = (
        jnp.dot(donor_rows, pair_weight, preferred_element_type=jnp.float32) * slot_w[:, None]
    )
    donor_term = lax.dot_general(
        weighted, pair_weight, (((1,), (1,)), ((), ())), preferred_element_type=jnp.float32
    ).astype(jnp.bfloat16)
    pair_part = lax.dot_general(
        donor_rows, weighted, (((0,), (0,)), ((), ())), preferred_element_type=jnp.float32
    )
    returned = lax.all_to_all(
        donor_term.reshape(seq_count, slot_count, channels),
        "seq",
        split_axis=0,
        concat_axis=0,
        tiled=True,
    )
    act_grad = (
        pooled.at[accept_index]
        .add(accept_term)
        .at[send_index]
        .add(returned.reshape(-1, channels).astype(jnp.float32))
    )
    conv_grad = (act_grad * slope).astype(jnp.bfloat16)
    padded = with_halo(conv_grad[None], (("seq", 1),), half)[0]
    piece = lax.all_gather(conv_weight, "dp", axis=1, tiled=True)
    total = jnp.zeros((slab_len, piece.shape[1]), jnp.float32)
    for tap in range(kernel):
        window = padded[2 * half - tap : 2 * half - tap + slab_len]
        total = total + lax.dot_general(
            window, piece[tap], (((1,), (1,)), ((), ())), preferred_element_type=jnp.float32
        )
    input_grad = total.astype(jnp.bfloat16)
    pair_sum = lax.psum(pair_part, ("dp", "seq"))
    scale = 1.0 / math.sqrt(lax.axis_size("dp") * seq_count * seq_count * slot_count)
    return (input_grad[None], pair_sum * scale)


MESH = pl.DeviceIdType.MESH
NZ, NY, NC = 4, 2, 2
Y_TAPS = 4
ROWS_T = (((0,), (0,)), ((), ()))
COLS_T = (((1,), (1,)), ((), ()))


def dot(a, b):
    return jnp.dot(a, b, preferred_element_type=jnp.float32)


def kernel(
    pre_hbm, trunk_ref, w_ref, p_hbm, ds_hbm, as_hbm, jg_hbm, pc_hbm,
    out_ref, pair_ref,
    pre_ref, p_ref, ds_ref, as_ref, jg_ref, pc_ref, trunk_mine, in_sem,
    act_s, slope_s, wbuf, trunk_in, dsend, drecv, tsend, trecv, drows, weighted_s, zbuf,
    pad_s, halo_send, halo_recv, part_s, c_send, c_recv, x_send, x_recv, own_s, r_send, r_recv,
    final,
    wz_s, wz_r, wy_s, wy_r, wx_s, wx_r, wc_s, wc_r, xs_s, xs_r, ar_s, ar_r, rs_s, rs_r, ag_s, ag_r,
):
    dp = lax.axis_index("dp")
    x = lax.axis_index("seq")
    c = dp % 2
    y = (dp // 2) % 2
    z = dp // 4
    me8 = dp // 2
    ox = 1 - x
    oc = 1 - c
    chan = pre_ref.shape[2]
    slots = ds_ref.shape[-1]
    shard = w_ref.shape[1]
    hc = chan // 2
    slab = pre_ref.shape[1]
    tok = slab // 2

    def dev(zz, yy, cc):
        return (zz * NY + yy) * NC + cc

    loads = [
        pltpu.make_async_copy(src, dst, in_sem.at[i])
        for i, (src, dst) in enumerate([
            (pre_hbm, pre_ref), (ds_hbm, ds_ref), (as_hbm, as_ref), (jg_hbm, jg_ref),
            (pc_hbm, pc_ref), (p_hbm, p_ref),
            (trunk_ref.at[0, pl.ds(pl.multiple_of(x * tok, 16), tok), :], trunk_mine)])
    ]
    for cp in loads:
        cp.start()

    def peer8(k):
        return lax.rem(me8 + k, 8)

    barrier = pltpu.get_barrier_semaphore()
    for k in range(1, 8):
        pl.semaphore_signal(barrier, inc=1, device_id=(peer8(k) * 2 + c, x), device_id_type=MESH)
    pl.semaphore_signal(barrier, inc=1, device_id=(me8 * 2 + oc, x), device_id_type=MESH)
    pl.semaphore_signal(barrier, inc=1, device_id=(dp, ox), device_id_type=MESH)
    pl.semaphore_wait(barrier, 9)

    def remote(src, dst, ss, rs, target):
        return pltpu.make_async_remote_copy(
            src_ref=src, dst_ref=dst, send_sem=ss, recv_sem=rs,
            device_id=target, device_id_type=MESH,
        )

    def wpart(ref, index, first_tap, taps):
        return ref.at[pl.ds(first_tap, taps), pl.ds(pl.multiple_of(index * shard, 16), shard), :]

    xdev = (dp, ox)
    cdev = (me8 * 2 + oc, x)
    ydev = (dev(z, 1 - y, c), x)
    taps = w_ref.shape[0]
    x_taps = taps - Y_TAPS

    trunk_copy = remote(
        trunk_ref.at[0, pl.ds(pl.multiple_of(ox * tok, 16), tok), :], trunk_in,
        xs_s.at[0], xs_r.at[0], xdev)
    trunk_copy.start()

    hops = [(d, s) for s in range(NZ - 1) for d in range(2)]

    def entry(hop):
        return 0 if hop is None else 1 + hop[0] * 3 + hop[1]

    def source_z(hop):
        if hop is None:
            return z
        return z - 1 - hop[1] if hop[0] == 0 else z + 1 + hop[1]

    def present(hop):
        return source_z(hop) >= 0 if hop[0] == 0 else source_z(hop) < NZ

    def when(hop, body):
        if hop is None:
            body()
        else:
            pl.when(present(hop))(body)

    def z_copy(d, s):
        block = wpart(wbuf, dev(z - s if d == 0 else z + s, y, c), 0, taps)
        return remote(w_ref if s == 0 else block, block, wz_s.at[d * 3 + s], wz_r.at[d * 3 + s],
                      (dev(z + 1 if d == 0 else z - 1, y, c), x))

    def z_arrival(d, s):
        block = wpart(wbuf, dev(source_z((d, s)), y, c), 0, taps)
        return remote(block, block, wz_s.at[d * 3 + s], wz_r.at[d * 3 + s], ydev)

    def has_next(d):
        return z < NZ - 1 if d == 0 else z > 0

    def y_copy(hop, arriving=False):
        index = dev(source_z(hop), 1 - y if arriving else y, c)
        block = wpart(wbuf, index, x * x_taps, Y_TAPS)
        src = w_ref.at[pl.ds(x * x_taps, Y_TAPS)] if hop is None and not arriving else block
        return remote(src, block, wy_s.at[entry(hop)], wy_r.at[entry(hop)], ydev)

    def x_copy_w(hop, arriving=False):
        start = (ox if arriving else x) * Y_TAPS
        block = wpart(wbuf, dev(source_z(hop), 1 - y, c), start, x_taps)
        return remote(block, block, wx_s.at[entry(hop)], wx_r.at[entry(hop)], xdev)

    def core_copy(kind, hop, arriving=False):
        yy, first_tap, count = [
            (y, 0, taps), (1 - y, x * x_taps, Y_TAPS), (1 - y, ox * Y_TAPS, x_taps)][kind]
        block = wpart(wbuf, dev(source_z(hop), yy, oc if arriving else c), first_tap, count)
        src = w_ref if kind == 0 and hop is None and not arriving else block
        sem = kind * 7 + entry(hop)
        return remote(src, block, wc_s.at[sem], wc_r.at[sem], cdev)

    for d in range(2):
        @pl.when(has_next(d))
        def _():
            z_copy(d, 0).start()
    y_copy(None).start()
    core_copy(0, None).start()
    own_w = pltpu.make_async_copy(w_ref, wpart(wbuf, dp, 0, taps), in_sem.at[7])
    own_w.start()

    def pass_z(s):
        for d in range(2):
            def body(d=d):
                z_arrival(d, s).wait_recv()
                if s < NZ - 2:
                    @pl.when(has_next(d))
                    def _():
                        z_copy(d, s + 1).start()
                y_copy((d, s)).start()
                core_copy(0, (d, s)).start()
            when((d, s), body)

    def pass_y(step):
        for hop in [None] if step == 0 else [(0, step - 1), (1, step - 1)]:
            def body(hop=hop):
                y_copy(hop, True).wait_recv()
                x_copy_w(hop).start()
                core_copy(1, hop).start()
            when(hop, body)

    def pass_x(step):
        for hop in [None] if step == 0 else [(0, step - 1), (1, step - 1)]:
            def body(hop=hop):
                x_copy_w(hop, True).wait_recv()
                core_copy(2, hop).start()
            when(hop, body)

    loads[0].wait()
    act_f, slope = gelu_parts(pre_ref[0].astype(jnp.float32))
    act_s[...] = act_f.astype(jnp.bfloat16)
    slope_s[...] = slope

    first = x == 0

    def loc_oth(rows):
        a, b = rows[0:1], rows[1:2]
        return jnp.where(first, a, b), jnp.where(first, b, a)

    for cp in loads[1:5]:
        cp.wait()
    d_loc, d_oth = loc_oth(ds_ref[0, 0])
    a_loc, a_oth = loc_oth(as_ref[0, 0])
    counts = pc_ref[0]
    cnt = jnp.where(first, counts[:, 0:1], counts[:, 1:2])
    live = lax.broadcasted_iota(jnp.int32, (2, slots), 1) < cnt
    w_loc, w_oth = loc_oth(jnp.where(live, jg_ref[0, 0], 0.0))

    position = lax.broadcasted_iota(jnp.int32, (slab, slots), 0)

    def onehot(row):
        return jnp.where(position == row, 1.0, 0.0)

    td_oth, td_loc, ta_oth, ta_loc = [onehot(r) for r in (d_oth, d_loc, a_oth, a_loc)]

    def flip(m):
        return jnp.transpose(m).astype(jnp.bfloat16)

    def column(row):
        return jnp.transpose(jnp.broadcast_to(row, (slots, slots)))[:, 0:1]

    dsend[...] = dot(flip(td_oth), act_s[...]).astype(jnp.bfloat16)
    d_copy = remote(dsend, drecv, xs_s.at[1], xs_r.at[1], xdev)
    d_copy.start()

    wc_oth, wc_loc = column(w_oth), column(w_loc)
    rows = dot(flip(ta_oth), act_s[...])
    weighted_s[0:slots, :] = (wc_oth * rows).astype(jnp.bfloat16)
    loads[5].wait()
    tsend[...] = lax.dot_general(
        weighted_s[0:slots, :], p_ref[...], COLS_T, preferred_element_type=jnp.float32
    ).astype(jnp.bfloat16)
    t_copy = remote(tsend, trecv, xs_s.at[2], xs_r.at[2], xdev)
    t_copy.start()

    pass_z(0)
    rows = dot(flip(ta_loc), act_s[...])
    weighted_s[slots:, :] = (wc_loc * rows).astype(jnp.bfloat16)
    zbuf[3 * slots : 4 * slots, :] = lax.dot_general(
        weighted_s[slots:, :], p_ref[...], COLS_T, preferred_element_type=jnp.float32
    ).astype(jnp.bfloat16)
    drows[slots:, :] = dot(flip(td_loc), act_s[...]).astype(jnp.bfloat16)
    zbuf[slots : 2 * slots, :] = (
        dot(drows[slots:, :], p_ref[...]) * wc_loc
    ).astype(jnp.bfloat16)

    d_copy.wait_recv()
    drows[0:slots, :] = drecv[...]
    part_s[...] = lax.dot_general(
        drows[...], weighted_s[...], ROWS_T, preferred_element_type=jnp.float32)
    c_send[...] = part_s[pl.ds(pl.multiple_of(oc * hc, 8), hc), :].astype(jnp.bfloat16)
    c_copy = remote(c_send, c_recv, ar_s.at[0], ar_r.at[0], cdev)
    c_copy.start()
    pass_y(0)
    zbuf[0:slots, :] = (dot(drows[0:slots, :], p_ref[...]) * wc_oth).astype(jnp.bfloat16)

    trunk_copy.wait_recv()
    loads[6].wait()
    mine = trunk_mine[...]
    zbuf[4 * slots :, 0:hc] = jnp.where(first, mine, trunk_in[...])
    zbuf[4 * slots :, hc:] = jnp.where(first, trunk_in[...], mine)
    t_copy.wait_recv()
    zbuf[2 * slots : 3 * slots, :] = trecv[...]
    spread = jnp.where(
        lax.broadcasted_iota(jnp.int32, (slab, tok), 0) // 2
        == lax.broadcasted_iota(jnp.int32, (slab, tok), 1), 0.5, 0.0)
    scatter = jnp.concatenate([ta_oth, ta_loc, td_oth, td_loc, spread], axis=1).astype(jnp.bfloat16)
    grad = (dot(scatter, zbuf[...]) * slope_s[...]).astype(jnp.bfloat16).astype(jnp.float32)
    pad_s[8 : 8 + slab, :] = grad
    halo_send[0:8, :] = grad[0:8]
    halo_send[8:16, :] = grad[slab - 8 : slab]
    h_copy = remote(halo_send, halo_recv, xs_s.at[3], xs_r.at[3], xdev)
    h_copy.start()

    pass_z(1)
    pass_x(0)
    c_copy.wait_recv()
    half = part_s[pl.ds(pl.multiple_of(c * hc, 8), hc), :] + c_recv[...].astype(jnp.float32)
    left, right = half[:, 0:hc], half[:, hc:]
    own_s[...] = jnp.where(first, left, right)
    x_send[...] = jnp.where(first, right, left).astype(jnp.bfloat16)
    x_copy = remote(x_send, x_recv, ar_s.at[1], ar_r.at[1], xdev)
    x_copy.start()

    pass_y(1)

    h_copy.wait_recv()
    nothing = jnp.zeros((8, chan), jnp.float32)
    pad_s[0:8, :] = jnp.where(first, nothing, halo_recv[8:16, :])
    pad_s[8 + slab :, :] = jnp.where(first, halo_recv[0:8, :], nothing)

    x_copy.wait_recv()
    own_s[...] = own_s[...] + x_recv[...].astype(jnp.float32)
    r_send[...] = own_s[...].astype(jnp.bfloat16)
    piece = hc // 8
    rs = []
    for k in range(1, 8):
        to = peer8(k)
        cp = remote(r_send.at[pl.ds(pl.multiple_of(to * piece, 16), piece), :], r_recv.at[k - 1],
                    rs_s.at[k - 1], rs_r.at[k - 1], (to * 2 + c, x))
        cp.start()
        rs.append(cp)

    pass_z(2)
    pass_x(1)
    pass_y(2)
    for cp in rs:
        cp.wait_recv()
    total = own_s[pl.ds(pl.multiple_of(me8 * piece, 8), piece), :]
    for k in range(7):
        total = total + r_recv[k].astype(jnp.float32)

    def fblock(cc, xx, start, size):
        return final.at[pl.ds(pl.multiple_of(cc * hc + start, 16), size),
                        pl.ds(pl.multiple_of(xx * hc, 128), hc)]

    r_done = r_send
    for cp in rs:
        cp.wait_send()
    r_done[0:piece, :] = total.astype(jnp.bfloat16)
    mine_to = pltpu.make_async_copy(
        r_done.at[0:piece, :], fblock(c, x, me8 * piece, piece), ar_s.at[5])
    mine_to.start()
    ag = []
    for k in range(1, 8):
        cp = remote(r_done.at[0:piece, :], fblock(c, x, me8 * piece, piece),
                    ag_s.at[k - 1], ag_r.at[k - 1], (peer8(k) * 2 + c, x))
        cp.start()
        ag.append(cp)

    mine_to.wait()
    for cp in ag:
        cp.wait_recv()
    quarter = fblock(c, x, 0, hc)
    xq = remote(quarter, quarter, ar_s.at[2], ar_r.at[2], xdev)
    xq.start()
    cq = remote(quarter, quarter, ar_s.at[3], ar_r.at[3], cdev)
    cq.start()
    pass_x(2)
    pass_y(3)
    pass_x(3)
    xq.wait_recv()
    other = fblock(c, ox, 0, hc)
    cq2 = remote(other, other, ar_s.at[4], ar_r.at[4], cdev)
    cq2.start()

    own_w.wait()
    for hop in [None] + hops:
        def arrived(hop=hop):
            for kind in range(3):
                core_copy(kind, hop, True).wait_recv()
        when(hop, arrived)
    kernel_w = w_ref.shape[0]
    shift = kernel_w // 2
    acc = None
    for tap in range(kernel_w):
        window = pad_s[8 + shift - tap : 8 + shift - tap + slab, :].astype(jnp.bfloat16)
        term = lax.dot_general(window, wbuf[tap], COLS_T, preferred_element_type=jnp.float32)
        acc = term if acc is None else acc + term
    out_ref[0] = acc.astype(jnp.bfloat16)

    cq.wait_recv()
    cq2.wait_recv()
    scale = 1.0 / math.sqrt(NZ * NY * NC * 2 * 2 * slots)
    pair_ref[...] = final[...].astype(jnp.float32) * scale
    for hop in [None] + hops:
        def sent(hop=hop):
            y_copy(hop).wait_send()
            x_copy_w(hop).wait_send()
            for kind in range(3):
                core_copy(kind, hop).wait_send()
        when(hop, sent)
    for d in range(2):
        for s in range(NZ - 1):
            leaves = (z < NZ - 1) & (z >= s) if d == 0 else (z > 0) & (z + s < NZ)
            @pl.when(leaves)
            def _(d=d, s=s):
                z_copy(d, s).wait_send()
    for cp in [trunk_copy, d_copy, t_copy, h_copy, c_copy, x_copy, xq, cq, cq2] + ag:
        cp.wait_send()


def per_device_kernel(pre_act, trunk_grad, conv_weight, pair_weight, donor_slots, accept_slots, junction_grad, pair_counts):
    slab, chan = pre_act.shape[1:]
    slots = donor_slots.shape[3]
    hc = chan // 2
    bf, f32 = jnp.bfloat16, jnp.float32
    V = pltpu.VMEM
    D = pltpu.SemaphoreType.DMA
    scratch = [
        V(pre_act.shape, bf), V(pair_weight.shape, bf), V(donor_slots.shape, jnp.int32),
        V(accept_slots.shape, jnp.int32), V(junction_grad.shape, f32), V(pair_counts.shape, jnp.int32),
        V((slab // 2, hc), bf), D((8,)),
        V((slab, chan), bf), V((slab, chan), f32), V((conv_weight.shape[0], chan, chan), bf),
        V((slab // 2, hc), bf), V((slots, chan), bf), V((slots, chan), bf),
        V((slots, chan), bf), V((slots, chan), bf), V((2 * slots, chan), bf),
        V((2 * slots, chan), bf), V((4 * slots + slab // 2, chan), bf),
        V((slab + 16, chan), f32), V((16, chan), f32), V((16, chan), f32),
        V((chan, chan), f32), V((hc, chan), bf), V((hc, chan), bf), V((hc, hc), bf), V((hc, hc), bf),
        V((hc, hc), f32), V((hc, hc), bf), V((7, hc // 8, hc), bf), V((chan, chan), bf),
        D((6,)), D((6,)), D((7,)), D((7,)), D((7,)), D((7,)), D((21,)), D((21,)), D((4,)), D((4,)),
        D((6,)), D((6,)), D((7,)), D((7,)), D((7,)), D((7,)),
    ]
    return pl.pallas_call(
        kernel,
        out_shape=(jax.ShapeDtypeStruct(pre_act.shape, bf), jax.ShapeDtypeStruct((chan, chan), f32)),
        in_specs=[pl.BlockSpec(memory_space=pltpu.HBM)] * 8,
        out_specs=[pl.BlockSpec(memory_space=pltpu.VMEM)] * 2,
        scratch_shapes=scratch,
        compiler_params=pltpu.CompilerParams(
            collective_id=0, has_side_effects=True, vmem_limit_bytes=60 << 20),
    )(pre_act, trunk_grad, conv_weight, pair_weight, donor_slots, accept_slots, junction_grad, pair_counts)


def solution(mesh):
    in_specs = (
        P("dp", "seq", None),
        P("dp", None, "seq"),
        P(None, "dp", None),
        P(),
        P("dp", "seq", None, None),
        P("dp", "seq", None, None),
        P("dp", "seq", None, None),
        P("dp", None, None),
    )
    out_specs = (P("dp", "seq", None), P())
    fits = mesh.shape["dp"] == NZ * NY * NC and mesh.shape["seq"] == 2
    return jax.shard_map(
        per_device_kernel if fits else per_device_general, mesh=mesh, in_specs=in_specs, out_specs=out_specs, check_vma=False
    )
```

```python
import math

import jax
import jax.numpy as jnp
from jax import lax
from jax.experimental import pallas as pl
from jax.experimental.pallas import tpu as pltpu
from jax.sharding import PartitionSpec as P


def with_halo(x, sides, width):
    for axis, dim in sides:
        size, length = (lax.axis_size(axis), x.shape[dim])
        up = [(i, (i + 1) % size) for i in range(size - 1)]
        down = [(j, i) for i, j in up]
        last = lax.slice_in_dim(x, length - width, length, axis=dim)
        first = lax.slice_in_dim(x, 0, width, axis=dim)
        before = lax.ppermute(last, axis, up)
        after = lax.ppermute(first, axis, down)
        x = jnp.concatenate([before, x, after], axis=dim)
    return x


def gelu_parts(values):
    normal_cdf = 0.5 * (1.0 + jax.scipy.special.erf(values / math.sqrt(2.0)))
    density = jnp.exp(-0.5 * values * values) / math.sqrt(2.0 * math.pi)
    return (values * normal_cdf, normal_cdf + values * density)


def per_device_general(
    pre_act,
    trunk_grad,
    conv_weight,
    pair_weight,
    donor_slots,
    accept_slots,
    junction_grad,
    pair_counts,
):
    seq_count = lax.axis_size("seq")
    my_slab = lax.axis_index("seq")
    slab_len = pre_act.shape[1]
    channels = pre_act.shape[2]
    slot_count = donor_slots.shape[3]
    kernel = conv_weight.shape[0]
    half = kernel // 2
    act_f, slope = gelu_parts(pre_act[0].astype(jnp.float32))
    act = act_f.astype(jnp.bfloat16)
    arrived = lax.all_to_all(trunk_grad, "seq", split_axis=1, concat_axis=2, tiled=True)
    pooled = jnp.repeat(arrived[0].astype(jnp.float32) * 0.5, 2, axis=0)
    send_index = donor_slots[0, 0].reshape(-1)
    outgoing = act[send_index].reshape(seq_count, slot_count, channels)
    incoming = lax.all_to_all(outgoing, "seq", split_axis=0, concat_axis=0, tiled=True)
    donor_rows = incoming.reshape(-1, channels)
    accept_index = accept_slots[0, 0].reshape(-1)
    counts_in = lax.dynamic_index_in_dim(pair_counts[0], my_slab, axis=1, keepdims=False)
    live = jnp.arange(slot_count, dtype=jnp.int32)[None, :] < counts_in[:, None]
    slot_w = jnp.where(live, junction_grad[0, 0], 0.0).reshape(-1)
    accept_rows = act[accept_index]
    weighted = (slot_w[:, None] * accept_rows.astype(jnp.float32)).astype(jnp.bfloat16)
    accept_term = (
        jnp.dot(donor_rows, pair_weight, preferred_element_type=jnp.float32) * slot_w[:, None]
    )
    donor_term = lax.dot_general(
        weighted, pair_weight, (((1,), (1,)), ((), ())), preferred_element_type=jnp.float32
    ).astype(jnp.bfloat16)
    pair_part = lax.dot_general(
        donor_rows, weighted, (((0,), (0,)), ((), ())), preferred_element_type=jnp.float32
    )
    returned = lax.all_to_all(
        donor_term.reshape(seq_count, slot_count, channels),
        "seq",
        split_axis=0,
        concat_axis=0,
        tiled=True,
    )
    act_grad = (
        pooled.at[accept_index]
        .add(accept_term)
        .at[send_index]
        .add(returned.reshape(-1, channels).astype(jnp.float32))
    )
    conv_grad = (act_grad * slope).astype(jnp.bfloat16)
    padded = with_halo(conv_grad[None], (("seq", 1),), half)[0]
    piece = lax.all_gather(conv_weight, "dp", axis=1, tiled=True)
    total = jnp.zeros((slab_len, piece.shape[1]), jnp.float32)
    for tap in range(kernel):
        window = padded[2 * half - tap : 2 * half - tap + slab_len]
        total = total + lax.dot_general(
            window, piece[tap], (((1,), (1,)), ((), ())), preferred_element_type=jnp.float32
        )
    input_grad = total.astype(jnp.bfloat16)
    pair_sum = lax.psum(pair_part, ("dp", "seq"))
    scale = 1.0 / math.sqrt(lax.axis_size("dp") * seq_count * seq_count * slot_count)
    return (input_grad[None], pair_sum * scale)


MESH = pl.DeviceIdType.MESH
NZ, NY, NC = 4, 2, 2
Y_TAPS = 4
ROWS_T = (((0,), (0,)), ((), ()))
COLS_T = (((1,), (1,)), ((), ()))


def dot(a, b):
    return jnp.dot(a, b, preferred_element_type=jnp.float32)


def kernel(
    pre_hbm, trunk_ref, w_ref, p_hbm, ds_hbm, as_hbm, jg_hbm, pc_hbm,
    out_ref, pair_ref,
    pre_ref, p_ref, ds_ref, as_ref, jg_ref, pc_ref, trunk_mine, in_sem,
    act_s, slope_s, wbuf, trunk_in, dsend, drecv, tsend, trecv, drows, weighted_s, zbuf,
    pad_s, halo_send, halo_recv, part_s, c_send, c_recv, x_send, x_recv, own_s, r_send, r_recv,
    final,
    wz_s, wz_r, wy_s, wy_r, wx_s, wx_r, wc_s, wc_r, xs_s, xs_r, ar_s, ar_r, rs_s, rs_r, ag_s, ag_r,
):
    dp = lax.axis_index("dp")
    x = lax.axis_index("seq")
    c = dp % 2
    y = (dp // 2) % 2
    z = dp // 4
    me8 = dp // 2
    ox = 1 - x
    oc = 1 - c
    chan = pre_ref.shape[2]
    slots = ds_ref.shape[-1]
    shard = w_ref.shape[1]
    hc = chan // 2
    slab = pre_ref.shape[1]
    tok = slab // 2

    def dev(zz, yy, cc):
        return (zz * NY + yy) * NC + cc

    loads = [
        pltpu.make_async_copy(src, dst, in_sem.at[i])
        for i, (src, dst) in enumerate([
            (pre_hbm, pre_ref), (ds_hbm, ds_ref), (as_hbm, as_ref), (jg_hbm, jg_ref),
            (pc_hbm, pc_ref), (p_hbm, p_ref),
            (trunk_ref.at[0, pl.ds(pl.multiple_of(x * tok, 16), tok), :], trunk_mine)])
    ]
    for cp in loads:
        cp.start()

    def peer8(k):
        return lax.rem(me8 + k, 8)

    barrier = pltpu.get_barrier_semaphore()
    for k in range(1, 8):
        pl.semaphore_signal(barrier, inc=1, device_id=(peer8(k) * 2 + c, x), device_id_type=MESH)
    pl.semaphore_signal(barrier, inc=1, device_id=(me8 * 2 + oc, x), device_id_type=MESH)
    pl.semaphore_signal(barrier, inc=1, device_id=(dp, ox), device_id_type=MESH)
    pl.semaphore_wait(barrier, 9)

    def remote(src, dst, ss, rs, target):
        return pltpu.make_async_remote_copy(
            src_ref=src, dst_ref=dst, send_sem=ss, recv_sem=rs,
            device_id=target, device_id_type=MESH,
        )

    def wpart(ref, index, first_tap, taps):
        return ref.at[pl.ds(first_tap, taps), pl.ds(pl.multiple_of(index * shard, 16), shard), :]

    xdev = (dp, ox)
    cdev = (me8 * 2 + oc, x)
    ydev = (dev(z, 1 - y, c), x)
    taps = w_ref.shape[0]
    x_taps = taps - Y_TAPS

    trunk_copy = remote(
        trunk_ref.at[0, pl.ds(pl.multiple_of(ox * tok, 16), tok), :], trunk_in,
        xs_s.at[0], xs_r.at[0], xdev)
    trunk_copy.start()

    hops = [(d, s) for s in range(NZ - 1) for d in range(2)]

    def entry(hop):
        return 0 if hop is None else 1 + hop[0] * 3 + hop[1]

    def source_z(hop):
        if hop is None:
            return z
        return z - 1 - hop[1] if hop[0] == 0 else z + 1 + hop[1]

    def present(hop):
        return source_z(hop) >= 0 if hop[0] == 0 else source_z(hop) < NZ

    def when(hop, body):
        if hop is None:
            body()
        else:
            pl.when(present(hop))(body)

    def z_copy(d, s):
        block = wpart(wbuf, dev(z - s if d == 0 else z + s, y, c), 0, taps)
        return remote(w_ref if s == 0 else block, block, wz_s.at[d * 3 + s], wz_r.at[d * 3 + s],
                      (dev(z + 1 if d == 0 else z - 1, y, c), x))

    def z_arrival(d, s):
        block = wpart(wbuf, dev(source_z((d, s)), y, c), 0, taps)
        return remote(block, block, wz_s.at[d * 3 + s], wz_r.at[d * 3 + s], ydev)

    def has_next(d):
        return z < NZ - 1 if d == 0 else z > 0

    def y_copy(hop, arriving=False):
        index = dev(source_z(hop), 1 - y if arriving else y, c)
        block = wpart(wbuf, index, x * x_taps, Y_TAPS)
        src = w_ref.at[pl.ds(x * x_taps, Y_TAPS)] if hop is None and not arriving else block
        return remote(src, block, wy_s.at[entry(hop)], wy_r.at[entry(hop)], ydev)

    def x_copy_w(hop, arriving=False):
        start = (ox if arriving else x) * Y_TAPS
        block = wpart(wbuf, dev(source_z(hop), 1 - y, c), start, x_taps)
        return remote(block, block, wx_s.at[entry(hop)], wx_r.at[entry(hop)], xdev)

    def core_copy(kind, hop, arriving=False):
        yy, first_tap, count = [
            (y, 0, taps), (1 - y, x * x_taps, Y_TAPS), (1 - y, ox * Y_TAPS, x_taps)][kind]
        block = wpart(wbuf, dev(source_z(hop), yy, oc if arriving else c), first_tap, count)
        src = w_ref if kind == 0 and hop is None and not arriving else block
        sem = kind * 7 + entry(hop)
        return remote(src, block, wc_s.at[sem], wc_r.at[sem], cdev)

    for d in range(2):
        @pl.when(has_next(d))
        def _():
            z_copy(d, 0).start()
    y_copy(None).start()
    core_copy(0, None).start()
    own_w = pltpu.make_async_copy(w_ref, wpart(wbuf, dp, 0, taps), in_sem.at[7])
    own_w.start()

    def pass_z(s):
        for d in range(2):
            def body(d=d):
                z_arrival(d, s).wait_recv()
                if s < NZ - 2:
                    @pl.when(has_next(d))
                    def _():
                        z_copy(d, s + 1).start()
                y_copy((d, s)).start()
                core_copy(0, (d, s)).start()
            when((d, s), body)

    def pass_y(step):
        for hop in [None] if step == 0 else [(0, step - 1), (1, step - 1)]:
            def body(hop=hop):
                y_copy(hop, True).wait_recv()
                x_copy_w(hop).start()
                core_copy(1, hop).start()
            when(hop, body)

    def pass_x(step):
        for hop in [None] if step == 0 else [(0, step - 1), (1, step - 1)]:
            def body(hop=hop):
                x_copy_w(hop, True).wait_recv()
                core_copy(2, hop).start()
            when(hop, body)

    loads[0].wait()
    values = pre_ref[0].astype(jnp.float32)
    normal_cdf = 0.5 * (1.0 + lax.erf(values / math.sqrt(2.0)))
    act_s[...] = (values * normal_cdf).astype(jnp.bfloat16)
    slope_s[...] = normal_cdf

    first = x == 0

    def loc_oth(rows):
        a, b = rows[0:1], rows[1:2]
        return jnp.where(first, a, b), jnp.where(first, b, a)

    for cp in loads[1:5]:
        cp.wait()
    d_loc, d_oth = loc_oth(ds_ref[0, 0])
    a_loc, a_oth = loc_oth(as_ref[0, 0])
    counts = pc_ref[0]
    cnt = jnp.where(first, counts[:, 0:1], counts[:, 1:2])
    live = lax.broadcasted_iota(jnp.int32, (2, slots), 1) < cnt
    w_loc, w_oth = loc_oth(jnp.where(live, jg_ref[0, 0], 0.0))

    position = lax.broadcasted_iota(jnp.int32, (slab, slots), 0)

    def onehot(row):
        return jnp.where(position == row, 1.0, 0.0)

    td_oth, td_loc, ta_oth, ta_loc = [onehot(r) for r in (d_oth, d_loc, a_oth, a_loc)]

    def flip(m):
        return jnp.transpose(m).astype(jnp.bfloat16)

    def column(row):
        return jnp.transpose(jnp.broadcast_to(row, (slots, slots)))[:, 0:1]

    dsend[...] = dot(flip(td_oth), act_s[...]).astype(jnp.bfloat16)
    d_copy = remote(dsend, drecv, xs_s.at[1], xs_r.at[1], xdev)
    d_copy.start()

    wc_oth, wc_loc = column(w_oth), column(w_loc)
    rows = dot(flip(ta_oth), act_s[...])
    weighted_s[0:slots, :] = (wc_oth * rows).astype(jnp.bfloat16)
    rows = dot(flip(ta_loc), act_s[...])
    weighted_s[slots:, :] = (wc_loc * rows).astype(jnp.bfloat16)
    drows[slots:, :] = dot(flip(td_loc), act_s[...]).astype(jnp.bfloat16)
    part_s[...] = lax.dot_general(
        drows[slots:, :], weighted_s[slots:, :], ROWS_T, preferred_element_type=jnp.float32)
    loads[5].wait()
    tsend[...] = lax.dot_general(
        weighted_s[0:slots, :], p_ref[...], COLS_T, preferred_element_type=jnp.float32
    ).astype(jnp.bfloat16)

    d_copy.wait_recv()
    t_copy = remote(tsend, trecv, xs_s.at[2], xs_r.at[2], xdev)
    t_copy.start()
    drows[0:slots, :] = drecv[...]
    part_s[...] += lax.dot_general(
        drows[0:slots, :], weighted_s[0:slots, :], ROWS_T, preferred_element_type=jnp.float32)
    c_send[...] = part_s[pl.ds(pl.multiple_of(oc * hc, 8), hc), :].astype(jnp.bfloat16)
    c_copy = remote(c_send, c_recv, ar_s.at[0], ar_r.at[0], cdev)
    c_copy.start()
    pass_z(0)
    zbuf[3 * slots : 4 * slots, :] = lax.dot_general(
        weighted_s[slots:, :], p_ref[...], COLS_T, preferred_element_type=jnp.float32
    ).astype(jnp.bfloat16)
    zbuf[0:slots, :] = (dot(drows[0:slots, :], p_ref[...]) * wc_oth).astype(jnp.bfloat16)
    zbuf[slots : 2 * slots, :] = (
        dot(drows[slots:, :], p_ref[...]) * wc_loc
    ).astype(jnp.bfloat16)
    pass_y(0)

    c_copy.wait_recv()
    half = part_s[pl.ds(pl.multiple_of(c * hc, 8), hc), :] + c_recv[...].astype(jnp.float32)
    left, right = half[:, 0:hc], half[:, hc:]
    x_send[...] = jnp.where(first, right, left).astype(jnp.bfloat16)
    x_copy = remote(x_send, x_recv, ar_s.at[1], ar_r.at[1], xdev)
    x_copy.start()
    own_s[...] = jnp.where(first, left, right)

    values = pre_ref[0].astype(jnp.float32)
    density = jnp.exp(-0.5 * values * values) / math.sqrt(2.0 * math.pi)
    slope_s[...] += values * density
    trunk_copy.wait_recv()
    loads[6].wait()
    mine = trunk_mine[...]
    zbuf[4 * slots :, 0:hc] = jnp.where(first, mine, trunk_in[...])
    zbuf[4 * slots :, hc:] = jnp.where(first, trunk_in[...], mine)
    t_copy.wait_recv()
    zbuf[2 * slots : 3 * slots, :] = trecv[...]
    spread = jnp.where(
        lax.broadcasted_iota(jnp.int32, (slab, tok), 0) // 2
        == lax.broadcasted_iota(jnp.int32, (slab, tok), 1), 0.5, 0.0)
    scatter = jnp.concatenate([ta_oth, ta_loc, td_oth, td_loc, spread], axis=1).astype(jnp.bfloat16)
    grad = (dot(scatter, zbuf[...]) * slope_s[...]).astype(jnp.bfloat16).astype(jnp.float32)
    pad_s[8 : 8 + slab, :] = grad
    halo_send[...] = jnp.where(first, grad[slab - 8 : slab], grad[0:8])
    h_copy = remote(halo_send, halo_recv, xs_s.at[3], xs_r.at[3], xdev)
    h_copy.start()

    pass_z(1)
    pass_x(0)
    x_copy.wait_recv()
    own_s[...] = own_s[...] + x_recv[...].astype(jnp.float32)
    r_send[...] = own_s[...].astype(jnp.bfloat16)
    piece = hc // 8
    rs = []
    for k in range(1, 8):
        to = peer8(k)
        cp = remote(r_send.at[pl.ds(pl.multiple_of(to * piece, 16), piece), :], r_recv.at[k - 1],
                    rs_s.at[k - 1], rs_r.at[k - 1], (to * 2 + c, x))
        cp.start()
        rs.append(cp)

    pass_y(1)
    h_copy.wait_recv()
    nothing = jnp.zeros((8, chan), jnp.float32)
    pad_s[0:8, :] = jnp.where(first, nothing, halo_recv[...])
    pad_s[8 + slab :, :] = jnp.where(first, halo_recv[...], nothing)

    pass_z(2)
    for cp in rs:
        cp.wait_recv()
    total = own_s[pl.ds(pl.multiple_of(me8 * piece, 8), piece), :]
    for k in range(7):
        total = total + r_recv[k].astype(jnp.float32)

    def fblock(cc, xx, start, size):
        return final.at[pl.ds(pl.multiple_of(cc * hc + start, 16), size),
                        pl.ds(pl.multiple_of(xx * hc, 128), hc)]

    r_done = r_send
    for cp in rs:
        cp.wait_send()
    r_done[0:piece, :] = total.astype(jnp.bfloat16)
    mine_to = pltpu.make_async_copy(
        r_done.at[0:piece, :], fblock(c, x, me8 * piece, piece), ar_s.at[5])
    mine_to.start()
    ag = []
    for k in range(1, 8):
        cp = remote(r_done.at[0:piece, :], fblock(c, x, me8 * piece, piece),
                    ag_s.at[k - 1], ag_r.at[k - 1], (peer8(k) * 2 + c, x))
        cp.start()
        ag.append(cp)

    pass_x(1)
    pass_y(2)
    mine_to.wait()
    for cp in ag:
        cp.wait_recv()
    quarter = fblock(c, x, 0, hc)
    xq = remote(quarter, quarter, ar_s.at[2], ar_r.at[2], xdev)
    xq.start()
    cq = remote(quarter, quarter, ar_s.at[3], ar_r.at[3], cdev)
    cq.start()
    pass_x(2)
    pass_y(3)
    pass_x(3)
    xq.wait_recv()
    other = fblock(c, ox, 0, hc)
    cq2 = remote(other, other, ar_s.at[4], ar_r.at[4], cdev)
    cq2.start()

    own_w.wait()
    for hop in [None] + hops:
        def arrived(hop=hop):
            for kind in range(3):
                core_copy(kind, hop, True).wait_recv()
        when(hop, arrived)
    kernel_w = w_ref.shape[0]
    shift = kernel_w // 2
    acc = None
    for tap in range(kernel_w):
        window = pad_s[8 + shift - tap : 8 + shift - tap + slab, :].astype(jnp.bfloat16)
        term = lax.dot_general(window, wbuf[tap], COLS_T, preferred_element_type=jnp.float32)
        acc = term if acc is None else acc + term
    out_ref[0] = acc.astype(jnp.bfloat16)

    cq.wait_recv()
    cq2.wait_recv()
    scale = 1.0 / math.sqrt(NZ * NY * NC * 2 * 2 * slots)
    pair_ref[...] = final[...].astype(jnp.float32) * scale
    for hop in [None] + hops:
        def sent(hop=hop):
            y_copy(hop).wait_send()
            x_copy_w(hop).wait_send()
            for kind in range(3):
                core_copy(kind, hop).wait_send()
        when(hop, sent)
    for d in range(2):
        for s in range(NZ - 1):
            leaves = (z < NZ - 1) & (z >= s) if d == 0 else (z > 0) & (z + s < NZ)
            @pl.when(leaves)
            def _(d=d, s=s):
                z_copy(d, s).wait_send()
    for cp in [trunk_copy, d_copy, t_copy, h_copy, c_copy, x_copy, xq, cq, cq2] + ag:
        cp.wait_send()


def per_device_kernel(pre_act, trunk_grad, conv_weight, pair_weight, donor_slots, accept_slots, junction_grad, pair_counts):
    slab, chan = pre_act.shape[1:]
    slots = donor_slots.shape[3]
    hc = chan // 2
    bf, f32 = jnp.bfloat16, jnp.float32
    V = pltpu.VMEM
    D = pltpu.SemaphoreType.DMA
    scratch = [
        V(pre_act.shape, bf), V(pair_weight.shape, bf), V(donor_slots.shape, jnp.int32),
        V(accept_slots.shape, jnp.int32), V(junction_grad.shape, f32), V(pair_counts.shape, jnp.int32),
        V((slab // 2, hc), bf), D((8,)),
        V((slab, chan), bf), V((slab, chan), f32), V((conv_weight.shape[0], chan, chan), bf),
        V((slab // 2, hc), bf), V((slots, chan), bf), V((slots, chan), bf),
        V((slots, chan), bf), V((slots, chan), bf), V((2 * slots, chan), bf),
        V((2 * slots, chan), bf), V((4 * slots + slab // 2, chan), bf),
        V((slab + 16, chan), f32), V((8, chan), f32), V((8, chan), f32),
        V((chan, chan), f32), V((hc, chan), bf), V((hc, chan), bf), V((hc, hc), bf), V((hc, hc), bf),
        V((hc, hc), f32), V((hc, hc), bf), V((7, hc // 8, hc), bf), V((chan, chan), bf),
        D((6,)), D((6,)), D((7,)), D((7,)), D((7,)), D((7,)), D((21,)), D((21,)), D((4,)), D((4,)),
        D((6,)), D((6,)), D((7,)), D((7,)), D((7,)), D((7,)),
    ]
    return pl.pallas_call(
        kernel,
        out_shape=(jax.ShapeDtypeStruct(pre_act.shape, bf), jax.ShapeDtypeStruct((chan, chan), f32)),
        in_specs=[pl.BlockSpec(memory_space=pltpu.HBM)] * 8,
        out_specs=[pl.BlockSpec(memory_space=pltpu.VMEM)] * 2,
        scratch_shapes=scratch,
        compiler_params=pltpu.CompilerParams(
            collective_id=0, has_side_effects=True, vmem_limit_bytes=40 << 20),
    )(*[
        pltpu.with_memory_space_constraint(a, pltpu.HBM)
        for a in (pre_act, trunk_grad, conv_weight, pair_weight, donor_slots, accept_slots,
                  junction_grad, pair_counts)
    ])


def solution(mesh):
    in_specs = (
        P("dp", "seq", None),
        P("dp", None, "seq"),
        P(None, "dp", None),
        P(),
        P("dp", "seq", None, None),
        P("dp", "seq", None, None),
        P("dp", "seq", None, None),
        P("dp", None, None),
    )
    out_specs = (P("dp", "seq", None), P())
    fits = mesh.shape["dp"] == NZ * NY * NC and mesh.shape["seq"] == 2
    return jax.shard_map(
        per_device_kernel if fits else per_device_general, mesh=mesh, in_specs=in_specs, out_specs=out_specs, check_vma=False
    )
```

```python
import math

import jax
import jax.numpy as jnp
from jax import lax
from jax.experimental import pallas as pl
from jax.experimental.pallas import tpu as pltpu
from jax.sharding import PartitionSpec as P


def with_halo(x, sides, width):
    for axis, dim in sides:
        size, length = (lax.axis_size(axis), x.shape[dim])
        up = [(i, (i + 1) % size) for i in range(size - 1)]
        down = [(j, i) for i, j in up]
        last = lax.slice_in_dim(x, length - width, length, axis=dim)
        first = lax.slice_in_dim(x, 0, width, axis=dim)
        before = lax.ppermute(last, axis, up)
        after = lax.ppermute(first, axis, down)
        x = jnp.concatenate([before, x, after], axis=dim)
    return x


def gelu_parts(values):
    normal_cdf = 0.5 * (1.0 + jax.scipy.special.erf(values / math.sqrt(2.0)))
    density = jnp.exp(-0.5 * values * values) / math.sqrt(2.0 * math.pi)
    return (values * normal_cdf, normal_cdf + values * density)


def per_device_general(
    pre_act,
    trunk_grad,
    conv_weight,
    pair_weight,
    donor_slots,
    accept_slots,
    junction_grad,
    pair_counts,
):
    seq_count = lax.axis_size("seq")
    my_slab = lax.axis_index("seq")
    slab_len = pre_act.shape[1]
    channels = pre_act.shape[2]
    slot_count = donor_slots.shape[3]
    kernel = conv_weight.shape[0]
    half = kernel // 2
    act_f, slope = gelu_parts(pre_act[0].astype(jnp.float32))
    act = act_f.astype(jnp.bfloat16)
    arrived = lax.all_to_all(trunk_grad, "seq", split_axis=1, concat_axis=2, tiled=True)
    pooled = jnp.repeat(arrived[0].astype(jnp.float32) * 0.5, 2, axis=0)
    send_index = donor_slots[0, 0].reshape(-1)
    outgoing = act[send_index].reshape(seq_count, slot_count, channels)
    incoming = lax.all_to_all(outgoing, "seq", split_axis=0, concat_axis=0, tiled=True)
    donor_rows = incoming.reshape(-1, channels)
    accept_index = accept_slots[0, 0].reshape(-1)
    counts_in = lax.dynamic_index_in_dim(pair_counts[0], my_slab, axis=1, keepdims=False)
    live = jnp.arange(slot_count, dtype=jnp.int32)[None, :] < counts_in[:, None]
    slot_w = jnp.where(live, junction_grad[0, 0], 0.0).reshape(-1)
    accept_rows = act[accept_index]
    weighted = (slot_w[:, None] * accept_rows.astype(jnp.float32)).astype(jnp.bfloat16)
    accept_term = (
        jnp.dot(donor_rows, pair_weight, preferred_element_type=jnp.float32) * slot_w[:, None]
    )
    donor_term = lax.dot_general(
        weighted, pair_weight, (((1,), (1,)), ((), ())), preferred_element_type=jnp.float32
    ).astype(jnp.bfloat16)
    pair_part = lax.dot_general(
        donor_rows, weighted, (((0,), (0,)), ((), ())), preferred_element_type=jnp.float32
    )
    returned = lax.all_to_all(
        donor_term.reshape(seq_count, slot_count, channels),
        "seq",
        split_axis=0,
        concat_axis=0,
        tiled=True,
    )
    act_grad = (
        pooled.at[accept_index]
        .add(accept_term)
        .at[send_index]
        .add(returned.reshape(-1, channels).astype(jnp.float32))
    )
    conv_grad = (act_grad * slope).astype(jnp.bfloat16)
    padded = with_halo(conv_grad[None], (("seq", 1),), half)[0]
    piece = lax.all_gather(conv_weight, "dp", axis=1, tiled=True)
    total = jnp.zeros((slab_len, piece.shape[1]), jnp.float32)
    for tap in range(kernel):
        window = padded[2 * half - tap : 2 * half - tap + slab_len]
        total = total + lax.dot_general(
            window, piece[tap], (((1,), (1,)), ((), ())), preferred_element_type=jnp.float32
        )
    input_grad = total.astype(jnp.bfloat16)
    pair_sum = lax.psum(pair_part, ("dp", "seq"))
    scale = 1.0 / math.sqrt(lax.axis_size("dp") * seq_count * seq_count * slot_count)
    return (input_grad[None], pair_sum * scale)


MESH = pl.DeviceIdType.MESH
NZ, NY, NC = 4, 2, 2
Y_TAPS = 4
ROWS_T = (((0,), (0,)), ((), ()))
COLS_T = (((1,), (1,)), ((), ()))


def dot(a, b):
    return jnp.dot(a, b, preferred_element_type=jnp.float32)


def kernel(
    pre_hbm, trunk_ref, w_ref, p_hbm, ds_hbm, as_hbm, jg_hbm, pc_hbm,
    out_ref, pair_ref,
    pre_ref, p_ref, ds_ref, as_ref, jg_ref, pc_ref, trunk_mine, in_sem,
    act_s, slope_s, wbuf, trunk_in, dsend, drecv, tsend, trecv, drows, weighted_s, zbuf,
    pad_s, halo_send, halo_recv, part_s, c_send, c_recv, x_send, x_recv, own_s, r_send, r_recv,
    final,
    wz_s, wz_r, wy_s, wy_r, wx_s, wx_r, wc_s, wc_r, xs_s, xs_r, ar_s, ar_r, rs_s, rs_r, ag_s, ag_r, xf_s, xf_r,
):
    dp = lax.axis_index("dp")
    x = lax.axis_index("seq")
    c = dp % 2
    y = (dp // 2) % 2
    z = dp // 4
    me8 = dp // 2
    ox = 1 - x
    oc = 1 - c
    chan = pre_ref.shape[2]
    slots = ds_ref.shape[-1]
    shard = w_ref.shape[1]
    hc = chan // 2
    slab = pre_ref.shape[1]
    tok = slab // 2

    def dev(zz, yy, cc):
        return (zz * NY + yy) * NC + cc

    loads = [
        pltpu.make_async_copy(src, dst, in_sem.at[i])
        for i, (src, dst) in enumerate([
            (pre_hbm, pre_ref), (ds_hbm, ds_ref), (as_hbm, as_ref), (jg_hbm, jg_ref),
            (pc_hbm, pc_ref), (p_hbm, p_ref),
            (trunk_ref.at[0, pl.ds(pl.multiple_of(x * tok, 16), tok), :], trunk_mine)])
    ]
    for cp in loads:
        cp.start()

    def peer8(k):
        return lax.rem(me8 + k, 8)

    barrier = pltpu.get_barrier_semaphore()
    for k in range(1, 8):
        pl.semaphore_signal(barrier, inc=1, device_id=(peer8(k) * 2 + c, x), device_id_type=MESH)
    pl.semaphore_signal(barrier, inc=1, device_id=(me8 * 2 + oc, x), device_id_type=MESH)
    pl.semaphore_signal(barrier, inc=1, device_id=(dp, ox), device_id_type=MESH)
    pl.semaphore_wait(barrier, 9)

    def remote(src, dst, ss, rs, target):
        return pltpu.make_async_remote_copy(
            src_ref=src, dst_ref=dst, send_sem=ss, recv_sem=rs,
            device_id=target, device_id_type=MESH,
        )

    def wpart(ref, index, first_tap, taps):
        return ref.at[pl.ds(first_tap, taps), pl.ds(pl.multiple_of(index * shard, 16), shard), :]

    xdev = (dp, ox)
    cdev = (me8 * 2 + oc, x)
    ydev = (dev(z, 1 - y, c), x)
    taps = w_ref.shape[0]
    x_taps = taps - Y_TAPS

    trunk_copy = remote(
        trunk_ref.at[0, pl.ds(pl.multiple_of(ox * tok, 16), tok), :], trunk_in,
        xs_s.at[0], xs_r.at[0], xdev)
    trunk_copy.start()

    hops = [(d, s) for s in range(NZ - 1) for d in range(2)]

    def entry(hop):
        return 0 if hop is None else 1 + hop[0] * 3 + hop[1]

    def source_z(hop):
        if hop is None:
            return z
        return z - 1 - hop[1] if hop[0] == 0 else z + 1 + hop[1]

    def present(hop):
        return source_z(hop) >= 0 if hop[0] == 0 else source_z(hop) < NZ

    def when(hop, body):
        if hop is None:
            body()
        else:
            pl.when(present(hop))(body)

    def z_copy(d, s):
        block = wpart(wbuf, dev(z - s if d == 0 else z + s, y, c), 0, taps)
        return remote(w_ref if s == 0 else block, block, wz_s.at[d * 3 + s], wz_r.at[d * 3 + s],
                      (dev(z + 1 if d == 0 else z - 1, y, c), x))

    def z_arrival(d, s):
        block = wpart(wbuf, dev(source_z((d, s)), y, c), 0, taps)
        return remote(block, block, wz_s.at[d * 3 + s], wz_r.at[d * 3 + s], ydev)

    def has_next(d):
        return z < NZ - 1 if d == 0 else z > 0

    def y_copy(hop, arriving=False):
        index = dev(source_z(hop), 1 - y if arriving else y, c)
        block = wpart(wbuf, index, x * x_taps, Y_TAPS)
        src = w_ref.at[pl.ds(x * x_taps, Y_TAPS)] if hop is None and not arriving else block
        return remote(src, block, wy_s.at[entry(hop)], wy_r.at[entry(hop)], ydev)

    def x_copy_w(hop, arriving=False):
        start = (ox if arriving else x) * Y_TAPS
        block = wpart(wbuf, dev(source_z(hop), 1 - y, c), start, x_taps)
        return remote(block, block, wx_s.at[entry(hop)], wx_r.at[entry(hop)], xdev)

    def core_copy(kind, hop, arriving=False):
        yy, first_tap, count = [
            (y, 0, taps), (1 - y, x * x_taps, Y_TAPS), (1 - y, ox * Y_TAPS, x_taps)][kind]
        block = wpart(wbuf, dev(source_z(hop), yy, oc if arriving else c), first_tap, count)
        src = w_ref if kind == 0 and hop is None and not arriving else block
        sem = kind * 7 + entry(hop)
        return remote(src, block, wc_s.at[sem], wc_r.at[sem], cdev)

    for d in range(2):
        @pl.when(has_next(d))
        def _():
            z_copy(d, 0).start()
    y_copy(None).start()
    core_copy(0, None).start()
    own_w = pltpu.make_async_copy(w_ref, wpart(wbuf, dp, 0, taps), in_sem.at[7])
    own_w.start()

    def pass_z(s):
        for d in range(2):
            def body(d=d):
                z_arrival(d, s).wait_recv()
                if s < NZ - 2:
                    @pl.when(has_next(d))
                    def _():
                        z_copy(d, s + 1).start()
                y_copy((d, s)).start()
                core_copy(0, (d, s)).start()
            when((d, s), body)

    def pass_y(step):
        for hop in [None] if step == 0 else [(0, step - 1), (1, step - 1)]:
            def body(hop=hop):
                y_copy(hop, True).wait_recv()
                x_copy_w(hop).start()
                core_copy(1, hop).start()
            when(hop, body)

    def pass_x(step):
        for hop in [None] if step == 0 else [(0, step - 1), (1, step - 1)]:
            def body(hop=hop):
                x_copy_w(hop, True).wait_recv()
                core_copy(2, hop).start()
            when(hop, body)

    loads[0].wait()
    values = pre_ref[0].astype(jnp.float32)
    normal_cdf = 0.5 * (1.0 + lax.erf(values / math.sqrt(2.0)))
    act_s[...] = (values * normal_cdf).astype(jnp.bfloat16)
    slope_s[...] = normal_cdf

    first = x == 0

    def loc_oth(rows):
        a, b = rows[0:1], rows[1:2]
        return jnp.where(first, a, b), jnp.where(first, b, a)

    for cp in loads[1:5]:
        cp.wait()
    d_loc, d_oth = loc_oth(ds_ref[0, 0])
    a_loc, a_oth = loc_oth(as_ref[0, 0])
    counts = pc_ref[0]
    cnt = jnp.where(first, counts[:, 0:1], counts[:, 1:2])
    live = lax.broadcasted_iota(jnp.int32, (2, slots), 1) < cnt
    w_loc, w_oth = loc_oth(jnp.where(live, jg_ref[0, 0], 0.0))

    position = lax.broadcasted_iota(jnp.int32, (slab, slots), 0)

    def onehot(row):
        return jnp.where(position == row, 1.0, 0.0)

    td_oth, td_loc, ta_oth, ta_loc = [onehot(r) for r in (d_oth, d_loc, a_oth, a_loc)]

    def flip(m):
        return jnp.transpose(m).astype(jnp.bfloat16)

    def column(row):
        return jnp.transpose(jnp.broadcast_to(row, (slots, slots)))[:, 0:1]

    dsend[...] = dot(flip(td_oth), act_s[...]).astype(jnp.bfloat16)
    d_copy = remote(dsend, drecv, xs_s.at[1], xs_r.at[1], xdev)
    d_copy.start()

    wc_oth, wc_loc = column(w_oth), column(w_loc)
    rows = dot(flip(ta_oth), act_s[...])
    weighted_s[0:slots, :] = (wc_oth * rows).astype(jnp.bfloat16)
    rows = dot(flip(ta_loc), act_s[...])
    weighted_s[slots:, :] = (wc_loc * rows).astype(jnp.bfloat16)
    drows[slots:, :] = dot(flip(td_loc), act_s[...]).astype(jnp.bfloat16)
    part_s[...] = lax.dot_general(
        drows[slots:, :], weighted_s[slots:, :], ROWS_T, preferred_element_type=jnp.float32)
    loads[5].wait()
    tsend[...] = lax.dot_general(
        weighted_s[0:slots, :], p_ref[...], COLS_T, preferred_element_type=jnp.float32
    ).astype(jnp.bfloat16)

    d_copy.wait_recv()
    t_copy = remote(tsend, trecv, xs_s.at[2], xs_r.at[2], xdev)
    t_copy.start()
    drows[0:slots, :] = drecv[...]
    part_s[...] += lax.dot_general(
        drows[0:slots, :], weighted_s[0:slots, :], ROWS_T, preferred_element_type=jnp.float32)
    given = part_s[pl.ds(pl.multiple_of(oc * hc, 8), hc), :]
    left, right = given[:, 0:hc], given[:, hc:]
    c_send[0] = jnp.where(first, right, left).astype(jnp.bfloat16)
    c_copy = remote(c_send.at[0], c_recv.at[0], ar_s.at[0], ar_r.at[0], cdev)
    c_copy.start()
    c_send[1] = jnp.where(first, left, right).astype(jnp.bfloat16)
    c_copy2 = remote(c_send.at[1], c_recv.at[1], ar_s.at[2], ar_r.at[2], cdev)
    c_copy2.start()
    pass_z(0)
    zbuf[3 * slots : 4 * slots, :] = lax.dot_general(
        weighted_s[slots:, :], p_ref[...], COLS_T, preferred_element_type=jnp.float32
    ).astype(jnp.bfloat16)
    zbuf[0:slots, :] = (dot(drows[0:slots, :], p_ref[...]) * wc_oth).astype(jnp.bfloat16)
    zbuf[slots : 2 * slots, :] = (
        dot(drows[slots:, :], p_ref[...]) * wc_loc
    ).astype(jnp.bfloat16)
    pass_y(0)

    c_copy.wait_recv()
    half = part_s[pl.ds(pl.multiple_of(c * hc, 8), hc), :]
    left, right = half[:, 0:hc], half[:, hc:]
    x_send[...] = (
        jnp.where(first, right, left) + c_recv[0].astype(jnp.float32)).astype(jnp.bfloat16)
    x_copy = remote(x_send, x_recv, ar_s.at[1], ar_r.at[1], xdev)
    x_copy.start()
    c_copy2.wait_recv()
    own_s[...] = jnp.where(first, left, right) + c_recv[1].astype(jnp.float32)

    values = pre_ref[0].astype(jnp.float32)
    density = jnp.exp(-0.5 * values * values) / math.sqrt(2.0 * math.pi)
    slope_s[...] += values * density
    trunk_copy.wait_recv()
    loads[6].wait()
    mine = trunk_mine[...]
    zbuf[4 * slots :, 0:hc] = jnp.where(first, mine, trunk_in[...])
    zbuf[4 * slots :, hc:] = jnp.where(first, trunk_in[...], mine)
    t_copy.wait_recv()
    zbuf[2 * slots : 3 * slots, :] = trecv[...]
    spread = jnp.where(
        lax.broadcasted_iota(jnp.int32, (slab, tok), 0) // 2
        == lax.broadcasted_iota(jnp.int32, (slab, tok), 1), 0.5, 0.0)
    scatter = jnp.concatenate([ta_oth, ta_loc, td_oth, td_loc, spread], axis=1).astype(jnp.bfloat16)
    grad = (dot(scatter, zbuf[...]) * slope_s[...]).astype(jnp.bfloat16).astype(jnp.float32)
    pad_s[8 : 8 + slab, :] = grad
    halo_send[...] = jnp.where(first, grad[slab - 8 : slab], grad[0:8])
    h_copy = remote(halo_send, halo_recv, xs_s.at[3], xs_r.at[3], xdev)
    h_copy.start()

    pass_z(1)
    pass_x(0)
    x_copy.wait_recv()
    own_s[...] = own_s[...] + x_recv[...].astype(jnp.float32)
    r_send[...] = own_s[...].astype(jnp.bfloat16)
    piece = hc // 8
    rs = []
    for k in range(1, 8):
        to = peer8(k)
        cp = remote(r_send.at[pl.ds(pl.multiple_of(to * piece, 16), piece), :], r_recv.at[k - 1],
                    rs_s.at[k - 1], rs_r.at[k - 1], (to * 2 + c, x))
        cp.start()
        rs.append(cp)

    pass_y(1)
    h_copy.wait_recv()
    nothing = jnp.zeros((8, chan), jnp.float32)
    pad_s[0:8, :] = jnp.where(first, nothing, halo_recv[...])
    pad_s[8 + slab :, :] = jnp.where(first, halo_recv[...], nothing)

    pass_z(2)
    for cp in rs:
        cp.wait_recv()
    total = own_s[pl.ds(pl.multiple_of(me8 * piece, 8), piece), :]
    for k in range(7):
        total = total + r_recv[k].astype(jnp.float32)

    def fblock(cc, xx, start, size):
        return final.at[pl.ds(pl.multiple_of(cc * hc + start, 16), size),
                        pl.ds(pl.multiple_of(xx * hc, 128), hc)]

    r_done = r_send
    for cp in rs:
        cp.wait_send()
    r_done[0:piece, :] = total.astype(jnp.bfloat16)
    mine_to = pltpu.make_async_copy(
        r_done.at[0:piece, :], fblock(c, x, me8 * piece, piece), ar_s.at[5])
    mine_to.start()
    ag = []
    for k in range(1, 8):
        cp = remote(r_done.at[0:piece, :], fblock(c, x, me8 * piece, piece),
                    ag_s.at[k - 1], ag_r.at[k - 1], (peer8(k) * 2 + c, x))
        cp.start()
        ag.append(cp)

    xf = [remote(r_done.at[0:piece, :], fblock(c, x, me8 * piece, piece),
                 xf_s.at[0], xf_r.at[0], xdev)]
    xf[0].start()
    for k in range(1, 8):
        ag[k - 1].wait_recv()
        block = fblock(c, x, lax.rem(me8 + 8 - k, 8) * piece, piece)
        cp = remote(block, block, xf_s.at[k], xf_r.at[k], xdev)
        cp.start()
        xf.append(cp)
    mine_to.wait()
    quarter = fblock(c, x, 0, hc)
    cq = remote(quarter, quarter, ar_s.at[3], ar_r.at[3], cdev)
    cq.start()
    pass_x(1)
    pass_y(2)
    pass_x(2)
    pass_y(3)
    pass_x(3)
    for cp in xf:
        cp.wait_recv()
    other = fblock(c, ox, 0, hc)
    cq2 = remote(other, other, ar_s.at[4], ar_r.at[4], cdev)
    cq2.start()

    own_w.wait()
    for hop in [None] + hops:
        def arrived(hop=hop):
            for kind in range(3):
                core_copy(kind, hop, True).wait_recv()
        when(hop, arrived)
    kernel_w = w_ref.shape[0]
    shift = kernel_w // 2
    acc = None
    for tap in range(kernel_w):
        window = pad_s[8 + shift - tap : 8 + shift - tap + slab, :].astype(jnp.bfloat16)
        term = lax.dot_general(window, wbuf[tap], COLS_T, preferred_element_type=jnp.float32)
        acc = term if acc is None else acc + term
    out_ref[0] = acc.astype(jnp.bfloat16)

    cq.wait_recv()
    cq2.wait_recv()
    scale = 1.0 / math.sqrt(NZ * NY * NC * 2 * 2 * slots)
    pair_ref[...] = final[...].astype(jnp.float32) * scale
    for hop in [None] + hops:
        def sent(hop=hop):
            y_copy(hop).wait_send()
            x_copy_w(hop).wait_send()
            for kind in range(3):
                core_copy(kind, hop).wait_send()
        when(hop, sent)
    for d in range(2):
        for s in range(NZ - 1):
            leaves = (z < NZ - 1) & (z >= s) if d == 0 else (z > 0) & (z + s < NZ)
            @pl.when(leaves)
            def _(d=d, s=s):
                z_copy(d, s).wait_send()
    for cp in [trunk_copy, d_copy, t_copy, h_copy, c_copy, c_copy2, x_copy, cq, cq2] + ag + xf:
        cp.wait_send()


def per_device_kernel(pre_act, trunk_grad, conv_weight, pair_weight, donor_slots, accept_slots, junction_grad, pair_counts):
    slab, chan = pre_act.shape[1:]
    slots = donor_slots.shape[3]
    hc = chan // 2
    bf, f32 = jnp.bfloat16, jnp.float32
    V = pltpu.VMEM
    D = pltpu.SemaphoreType.DMA
    scratch = [
        V(pre_act.shape, bf), V(pair_weight.shape, bf), V(donor_slots.shape, jnp.int32),
        V(accept_slots.shape, jnp.int32), V(junction_grad.shape, f32), V(pair_counts.shape, jnp.int32),
        V((slab // 2, hc), bf), D((8,)),
        V((slab, chan), bf), V((slab, chan), f32), V((conv_weight.shape[0], chan, chan), bf),
        V((slab // 2, hc), bf), V((slots, chan), bf), V((slots, chan), bf),
        V((slots, chan), bf), V((slots, chan), bf), V((2 * slots, chan), bf),
        V((2 * slots, chan), bf), V((4 * slots + slab // 2, chan), bf),
        V((slab + 16, chan), f32), V((8, chan), f32), V((8, chan), f32),
        V((chan, chan), f32), V((2, hc, hc), bf), V((2, hc, hc), bf), V((hc, hc), bf), V((hc, hc), bf),
        V((hc, hc), f32), V((hc, hc), bf), V((7, hc // 8, hc), bf), V((chan, chan), bf),
        D((6,)), D((6,)), D((7,)), D((7,)), D((7,)), D((7,)), D((21,)), D((21,)), D((4,)), D((4,)),
        D((6,)), D((6,)), D((7,)), D((7,)), D((7,)), D((7,)), D((8,)), D((8,)),
    ]
    return pl.pallas_call(
        kernel,
        out_shape=(jax.ShapeDtypeStruct(pre_act.shape, bf), jax.ShapeDtypeStruct((chan, chan), f32)),
        in_specs=[pl.BlockSpec(memory_space=pltpu.HBM)] * 8,
        out_specs=[pl.BlockSpec(memory_space=pltpu.VMEM)] * 2,
        scratch_shapes=scratch,
        compiler_params=pltpu.CompilerParams(
            collective_id=0, has_side_effects=True, vmem_limit_bytes=40 << 20),
    )(*[
        pltpu.with_memory_space_constraint(a, pltpu.HBM)
        for a in (pre_act, trunk_grad, conv_weight, pair_weight, donor_slots, accept_slots,
                  junction_grad, pair_counts)
    ])


def solution(mesh):
    in_specs = (
        P("dp", "seq", None),
        P("dp", None, "seq"),
        P(None, "dp", None),
        P(),
        P("dp", "seq", None, None),
        P("dp", "seq", None, None),
        P("dp", "seq", None, None),
        P("dp", None, None),
    )
    out_specs = (P("dp", "seq", None), P())
    fits = mesh.shape["dp"] == NZ * NY * NC and mesh.shape["seq"] == 2
    return jax.shard_map(
        per_device_kernel if fits else per_device_general, mesh=mesh, in_specs=in_specs, out_specs=out_specs, check_vma=False
    )
```

```python
import math

import jax
import jax.numpy as jnp
from jax import lax
from jax.experimental import pallas as pl
from jax.experimental.pallas import tpu as pltpu
from jax.sharding import PartitionSpec as P


def with_halo(x, sides, width):
    for axis, dim in sides:
        size, length = (lax.axis_size(axis), x.shape[dim])
        up = [(i, (i + 1) % size) for i in range(size - 1)]
        down = [(j, i) for i, j in up]
        last = lax.slice_in_dim(x, length - width, length, axis=dim)
        first = lax.slice_in_dim(x, 0, width, axis=dim)
        before = lax.ppermute(last, axis, up)
        after = lax.ppermute(first, axis, down)
        x = jnp.concatenate([before, x, after], axis=dim)
    return x


def gelu_parts(values):
    normal_cdf = 0.5 * (1.0 + jax.scipy.special.erf(values / math.sqrt(2.0)))
    density = jnp.exp(-0.5 * values * values) / math.sqrt(2.0 * math.pi)
    return (values * normal_cdf, normal_cdf + values * density)


def per_device_general(
    pre_act,
    trunk_grad,
    conv_weight,
    pair_weight,
    donor_slots,
    accept_slots,
    junction_grad,
    pair_counts,
):
    seq_count = lax.axis_size("seq")
    my_slab = lax.axis_index("seq")
    slab_len = pre_act.shape[1]
    channels = pre_act.shape[2]
    slot_count = donor_slots.shape[3]
    kernel = conv_weight.shape[0]
    half = kernel // 2
    act_f, slope = gelu_parts(pre_act[0].astype(jnp.float32))
    act = act_f.astype(jnp.bfloat16)
    arrived = lax.all_to_all(trunk_grad, "seq", split_axis=1, concat_axis=2, tiled=True)
    pooled = jnp.repeat(arrived[0].astype(jnp.float32) * 0.5, 2, axis=0)
    send_index = donor_slots[0, 0].reshape(-1)
    outgoing = act[send_index].reshape(seq_count, slot_count, channels)
    incoming = lax.all_to_all(outgoing, "seq", split_axis=0, concat_axis=0, tiled=True)
    donor_rows = incoming.reshape(-1, channels)
    accept_index = accept_slots[0, 0].reshape(-1)
    counts_in = lax.dynamic_index_in_dim(pair_counts[0], my_slab, axis=1, keepdims=False)
    live = jnp.arange(slot_count, dtype=jnp.int32)[None, :] < counts_in[:, None]
    slot_w = jnp.where(live, junction_grad[0, 0], 0.0).reshape(-1)
    accept_rows = act[accept_index]
    weighted = (slot_w[:, None] * accept_rows.astype(jnp.float32)).astype(jnp.bfloat16)
    accept_term = (
        jnp.dot(donor_rows, pair_weight, preferred_element_type=jnp.float32) * slot_w[:, None]
    )
    donor_term = lax.dot_general(
        weighted, pair_weight, (((1,), (1,)), ((), ())), preferred_element_type=jnp.float32
    ).astype(jnp.bfloat16)
    pair_part = lax.dot_general(
        donor_rows, weighted, (((0,), (0,)), ((), ())), preferred_element_type=jnp.float32
    )
    returned = lax.all_to_all(
        donor_term.reshape(seq_count, slot_count, channels),
        "seq",
        split_axis=0,
        concat_axis=0,
        tiled=True,
    )
    act_grad = (
        pooled.at[accept_index]
        .add(accept_term)
        .at[send_index]
        .add(returned.reshape(-1, channels).astype(jnp.float32))
    )
    conv_grad = (act_grad * slope).astype(jnp.bfloat16)
    padded = with_halo(conv_grad[None], (("seq", 1),), half)[0]
    piece = lax.all_gather(conv_weight, "dp", axis=1, tiled=True)
    total = jnp.zeros((slab_len, piece.shape[1]), jnp.float32)
    for tap in range(kernel):
        window = padded[2 * half - tap : 2 * half - tap + slab_len]
        total = total + lax.dot_general(
            window, piece[tap], (((1,), (1,)), ((), ())), preferred_element_type=jnp.float32
        )
    input_grad = total.astype(jnp.bfloat16)
    pair_sum = lax.psum(pair_part, ("dp", "seq"))
    scale = 1.0 / math.sqrt(lax.axis_size("dp") * seq_count * seq_count * slot_count)
    return (input_grad[None], pair_sum * scale)


MESH = pl.DeviceIdType.MESH
NZ, NY, NC = 4, 2, 2
Y_TAPS = 4
ROWS_T = (((0,), (0,)), ((), ()))
COLS_T = (((1,), (1,)), ((), ()))


def dot(a, b):
    return jnp.dot(a, b, preferred_element_type=jnp.float32)


def kernel(
    pre_hbm, trunk_ref, w_ref, p_hbm, ds_hbm, as_hbm, jg_hbm, pc_hbm,
    out_ref, pair_ref,
    pre_ref, p_ref, ds_ref, as_ref, jg_ref, pc_ref, trunk_mine, in_sem,
    act_s, slope_s, wbuf, trunk_in, dsend, drecv, tsend, trecv, drows, weighted_s, zbuf,
    pad_s, halo_send, halo_recv, part_s, c_send, c_recv, x_send, x_recv, own_s, r_send, r_recv,
    final,
    wz_s, wz_r, wy_s, wy_r, wx_s, wx_r, wc_s, wc_r, xs_s, xs_r, ar_s, ar_r, rs_s, rs_r, ag_s, ag_r, xf_s, xf_r,
):
    dp = lax.axis_index("dp")
    x = lax.axis_index("seq")
    c = dp % 2
    y = (dp // 2) % 2
    z = dp // 4
    me8 = dp // 2
    ox = 1 - x
    oc = 1 - c
    chan = pre_ref.shape[2]
    slots = ds_ref.shape[-1]
    shard = w_ref.shape[1]
    hc = chan // 2
    slab = pre_ref.shape[1]
    tok = slab // 2

    def dev(zz, yy, cc):
        return (zz * NY + yy) * NC + cc

    loads = [
        pltpu.make_async_copy(src, dst, in_sem.at[i])
        for i, (src, dst) in enumerate([
            (pre_hbm, pre_ref), (ds_hbm, ds_ref), (as_hbm, as_ref), (jg_hbm, jg_ref),
            (pc_hbm, pc_ref), (p_hbm, p_ref),
            (trunk_ref.at[0, pl.ds(pl.multiple_of(x * tok, 16), tok), :], trunk_mine)])
    ]
    for cp in loads:
        cp.start()

    def peer8(k):
        return lax.rem(me8 + k, 8)

    barrier = pltpu.get_barrier_semaphore()
    for k in range(1, 8):
        pl.semaphore_signal(barrier, inc=1, device_id=(peer8(k) * 2 + c, x), device_id_type=MESH)
    pl.semaphore_signal(barrier, inc=1, device_id=(me8 * 2 + oc, x), device_id_type=MESH)
    pl.semaphore_signal(barrier, inc=1, device_id=(dp, ox), device_id_type=MESH)
    pl.semaphore_wait(barrier, 9)

    def remote(src, dst, ss, rs, target):
        return pltpu.make_async_remote_copy(
            src_ref=src, dst_ref=dst, send_sem=ss, recv_sem=rs,
            device_id=target, device_id_type=MESH,
        )

    def wpart(ref, index, first_tap, taps):
        return ref.at[pl.ds(first_tap, taps), pl.ds(pl.multiple_of(index * shard, 16), shard), :]

    xdev = (dp, ox)
    cdev = (me8 * 2 + oc, x)
    ydev = (dev(z, 1 - y, c), x)
    taps = w_ref.shape[0]
    x_taps = taps - Y_TAPS

    trunk_copy = remote(
        trunk_ref.at[0, pl.ds(pl.multiple_of(ox * tok, 16), tok), :], trunk_in,
        xs_s.at[0], xs_r.at[0], xdev)
    trunk_copy.start()

    hops = [(d, s) for s in range(NZ - 1) for d in range(2)]

    def entry(hop):
        return 0 if hop is None else 1 + hop[0] * 3 + hop[1]

    def source_z(hop):
        if hop is None:
            return z
        return z - 1 - hop[1] if hop[0] == 0 else z + 1 + hop[1]

    def present(hop):
        return source_z(hop) >= 0 if hop[0] == 0 else source_z(hop) < NZ

    def when(hop, body):
        if hop is None:
            body()
        else:
            pl.when(present(hop))(body)

    def z_copy(d, s):
        block = wpart(wbuf, dev(z - s if d == 0 else z + s, y, c), 0, taps)
        return remote(w_ref if s == 0 else block, block, wz_s.at[d * 3 + s], wz_r.at[d * 3 + s],
                      (dev(z + 1 if d == 0 else z - 1, y, c), x))

    def z_arrival(d, s):
        block = wpart(wbuf, dev(source_z((d, s)), y, c), 0, taps)
        return remote(block, block, wz_s.at[d * 3 + s], wz_r.at[d * 3 + s], ydev)

    def has_next(d):
        return z < NZ - 1 if d == 0 else z > 0

    def y_copy(hop, arriving=False):
        index = dev(source_z(hop), 1 - y if arriving else y, c)
        block = wpart(wbuf, index, x * x_taps, Y_TAPS)
        src = w_ref.at[pl.ds(x * x_taps, Y_TAPS)] if hop is None and not arriving else block
        return remote(src, block, wy_s.at[entry(hop)], wy_r.at[entry(hop)], ydev)

    def x_copy_w(hop, arriving=False):
        start = (ox if arriving else x) * Y_TAPS
        block = wpart(wbuf, dev(source_z(hop), 1 - y, c), start, x_taps)
        return remote(block, block, wx_s.at[entry(hop)], wx_r.at[entry(hop)], xdev)

    def core_copy(kind, hop, arriving=False):
        yy, first_tap, count = [
            (y, 0, taps), (1 - y, x * x_taps, Y_TAPS), (1 - y, ox * Y_TAPS, x_taps)][kind]
        block = wpart(wbuf, dev(source_z(hop), yy, oc if arriving else c), first_tap, count)
        src = w_ref if kind == 0 and hop is None and not arriving else block
        sem = kind * 7 + entry(hop)
        return remote(src, block, wc_s.at[sem], wc_r.at[sem], cdev)

    for d in range(2):
        @pl.when(has_next(d))
        def _():
            z_copy(d, 0).start()
    y_copy(None).start()
    core_copy(0, None).start()
    own_w = pltpu.make_async_copy(w_ref, wpart(wbuf, dp, 0, taps), in_sem.at[7])
    own_w.start()

    def pass_z(s):
        for d in range(2):
            def body(d=d):
                z_arrival(d, s).wait_recv()
                if s < NZ - 2:
                    @pl.when(has_next(d))
                    def _():
                        z_copy(d, s + 1).start()
                y_copy((d, s)).start()
                core_copy(0, (d, s)).start()
            when((d, s), body)

    def pass_y(step):
        for hop in [None] if step == 0 else [(0, step - 1), (1, step - 1)]:
            def body(hop=hop):
                y_copy(hop, True).wait_recv()
                x_copy_w(hop).start()
                core_copy(1, hop).start()
            when(hop, body)

    def pass_x(step):
        for hop in [None] if step == 0 else [(0, step - 1), (1, step - 1)]:
            def body(hop=hop):
                x_copy_w(hop, True).wait_recv()
                core_copy(2, hop).start()
            when(hop, body)

    loads[0].wait()
    values = pre_ref[0].astype(jnp.float32)
    normal_cdf = 0.5 * (1.0 + lax.erf(values / math.sqrt(2.0)))
    act_s[...] = (values * normal_cdf).astype(jnp.bfloat16)
    slope_s[...] = normal_cdf

    first = x == 0

    def loc_oth(rows):
        a, b = rows[0:1], rows[1:2]
        return jnp.where(first, a, b), jnp.where(first, b, a)

    for cp in loads[1:5]:
        cp.wait()
    d_loc, d_oth = loc_oth(ds_ref[0, 0])
    a_loc, a_oth = loc_oth(as_ref[0, 0])
    counts = pc_ref[0]
    cnt = jnp.where(first, counts[:, 0:1], counts[:, 1:2])
    live = lax.broadcasted_iota(jnp.int32, (2, slots), 1) < cnt
    w_loc, w_oth = loc_oth(jnp.where(live, jg_ref[0, 0], 0.0))

    position = lax.broadcasted_iota(jnp.int32, (slab, slots), 0)

    def onehot(row):
        return jnp.where(position == row, 1.0, 0.0)

    td_oth, td_loc, ta_oth, ta_loc = [onehot(r) for r in (d_oth, d_loc, a_oth, a_loc)]

    def flip(m):
        return jnp.transpose(m).astype(jnp.bfloat16)

    def column(row):
        return jnp.transpose(jnp.broadcast_to(row, (slots, slots)))[:, 0:1]

    dsend[...] = dot(flip(td_oth), act_s[...]).astype(jnp.bfloat16)
    d_copy = remote(dsend, drecv, xs_s.at[1], xs_r.at[1], xdev)
    d_copy.start()

    wc_oth, wc_loc = column(w_oth), column(w_loc)
    rows = dot(flip(ta_oth), act_s[...])
    weighted_s[0:slots, :] = (wc_oth * rows).astype(jnp.bfloat16)
    rows = dot(flip(ta_loc), act_s[...])
    weighted_s[slots:, :] = (wc_loc * rows).astype(jnp.bfloat16)
    drows[slots:, :] = dot(flip(td_loc), act_s[...]).astype(jnp.bfloat16)
    part_s[...] = lax.dot_general(
        drows[slots:, :], weighted_s[slots:, :], ROWS_T, preferred_element_type=jnp.float32)
    loads[5].wait()
    tsend[...] = lax.dot_general(
        weighted_s[0:slots, :], p_ref[...], COLS_T, preferred_element_type=jnp.float32
    ).astype(jnp.bfloat16)

    d_copy.wait_recv()
    t_copy = remote(tsend, trecv, xs_s.at[2], xs_r.at[2], xdev)
    t_copy.start()
    drows[0:slots, :] = drecv[...]
    part_s[...] += lax.dot_general(
        drows[0:slots, :], weighted_s[0:slots, :], ROWS_T, preferred_element_type=jnp.float32)
    given = part_s[pl.ds(pl.multiple_of(oc * hc, 8), hc), :]
    left, right = given[:, 0:hc], given[:, hc:]
    c_send[0] = jnp.where(first, right, left).astype(jnp.bfloat16)
    c_copy = remote(c_send.at[0], c_recv.at[0], ar_s.at[0], ar_r.at[0], cdev)
    c_copy.start()
    c_send[1] = jnp.where(first, left, right).astype(jnp.bfloat16)
    c_copy2 = remote(c_send.at[1], c_recv.at[1], ar_s.at[2], ar_r.at[2], cdev)
    c_copy2.start()
    pass_z(0)
    zbuf[3 * slots : 4 * slots, :] = lax.dot_general(
        weighted_s[slots:, :], p_ref[...], COLS_T, preferred_element_type=jnp.float32
    ).astype(jnp.bfloat16)
    zbuf[0:slots, :] = (dot(drows[0:slots, :], p_ref[...]) * wc_oth).astype(jnp.bfloat16)
    zbuf[slots : 2 * slots, :] = (
        dot(drows[slots:, :], p_ref[...]) * wc_loc
    ).astype(jnp.bfloat16)
    pass_y(0)

    c_copy.wait_recv()
    half = part_s[pl.ds(pl.multiple_of(c * hc, 8), hc), :]
    left, right = half[:, 0:hc], half[:, hc:]
    x_send[...] = (
        jnp.where(first, right, left) + c_recv[0].astype(jnp.float32)).astype(jnp.bfloat16)
    x_copy = remote(x_send, x_recv, ar_s.at[1], ar_r.at[1], xdev)
    x_copy.start()
    c_copy2.wait_recv()
    own_s[...] = jnp.where(first, left, right) + c_recv[1].astype(jnp.float32)

    values = pre_ref[0].astype(jnp.float32)
    density = jnp.exp(-0.5 * values * values) / math.sqrt(2.0 * math.pi)
    slope_s[...] += values * density
    trunk_copy.wait_recv()
    loads[6].wait()
    mine = trunk_mine[...]
    zbuf[4 * slots :, 0:hc] = jnp.where(first, mine, trunk_in[...])
    zbuf[4 * slots :, hc:] = jnp.where(first, trunk_in[...], mine)
    t_copy.wait_recv()
    zbuf[2 * slots : 3 * slots, :] = trecv[...]
    spread = jnp.where(
        lax.broadcasted_iota(jnp.int32, (slab, tok), 0) // 2
        == lax.broadcasted_iota(jnp.int32, (slab, tok), 1), 0.5, 0.0)
    scatter = jnp.concatenate([ta_oth, ta_loc, td_oth, td_loc, spread], axis=1).astype(jnp.bfloat16)
    grad = (dot(scatter, zbuf[...]) * slope_s[...]).astype(jnp.bfloat16).astype(jnp.float32)
    pad_s[8 : 8 + slab, :] = grad
    halo_send[...] = jnp.where(first, grad[slab - 8 : slab], grad[0:8])
    h_copy = remote(halo_send, halo_recv, xs_s.at[3], xs_r.at[3], xdev)
    h_copy.start()

    pass_z(1)
    pass_x(0)
    x_copy.wait_recv()
    own_s[...] = own_s[...] + x_recv[...].astype(jnp.float32)
    r_send[...] = own_s[...].astype(jnp.bfloat16)
    piece = hc // 8
    rs = []
    for k in range(1, 8):
        to = peer8(k)
        cp = remote(r_send.at[pl.ds(pl.multiple_of(to * piece, 16), piece), :], r_recv.at[k - 1],
                    rs_s.at[k - 1], rs_r.at[k - 1], (to * 2 + c, x))
        cp.start()
        rs.append(cp)

    pass_y(1)
    h_copy.wait_recv()
    nothing = jnp.zeros((8, chan), jnp.float32)
    pad_s[0:8, :] = jnp.where(first, nothing, halo_recv[...])
    pad_s[8 + slab :, :] = jnp.where(first, halo_recv[...], nothing)

    pass_z(2)
    for cp in rs:
        cp.wait_recv()
    total = own_s[pl.ds(pl.multiple_of(me8 * piece, 8), piece), :]
    for k in range(7):
        total = total + r_recv[k].astype(jnp.float32)

    def fblock(cc, xx, start, size):
        return final.at[pl.ds(pl.multiple_of(cc * hc + start, 16), size),
                        pl.ds(pl.multiple_of(xx * hc, 128), hc)]

    r_done = r_send
    for cp in rs:
        cp.wait_send()
    r_done[0:piece, :] = total.astype(jnp.bfloat16)
    mine_to = pltpu.make_async_copy(
        r_done.at[0:piece, :], fblock(c, x, me8 * piece, piece), ar_s.at[5])
    mine_to.start()
    ag = []
    for k in range(1, 8):
        cp = remote(r_done.at[0:piece, :], fblock(c, x, me8 * piece, piece),
                    ag_s.at[k - 1], ag_r.at[k - 1], (peer8(k) * 2 + c, x))
        cp.start()
        ag.append(cp)

    pass_x(1)
    pass_y(2)
    xf = [remote(r_done.at[0:piece, :], fblock(c, x, me8 * piece, piece),
                 xf_s.at[0], xf_r.at[0], xdev)]
    xf[0].start()
    for k in range(1, 8):
        ag[k - 1].wait_recv()
        block = fblock(c, x, lax.rem(me8 + 8 - k, 8) * piece, piece)
        cp = remote(block, block, xf_s.at[k], xf_r.at[k], xdev)
        cp.start()
        xf.append(cp)
    mine_to.wait()
    quarter = fblock(c, x, 0, hc)
    cq = remote(quarter, quarter, ar_s.at[3], ar_r.at[3], cdev)
    cq.start()
    pass_x(2)
    pass_y(3)
    pass_x(3)
    for cp in xf:
        cp.wait_recv()
    other = fblock(c, ox, 0, hc)
    cq2 = remote(other, other, ar_s.at[4], ar_r.at[4], cdev)
    cq2.start()

    own_w.wait()
    for hop in [None] + hops:
        def arrived(hop=hop):
            for kind in range(3):
                core_copy(kind, hop, True).wait_recv()
        when(hop, arrived)
    kernel_w = w_ref.shape[0]
    shift = kernel_w // 2
    acc = None
    for tap in range(kernel_w):
        window = pad_s[8 + shift - tap : 8 + shift - tap + slab, :].astype(jnp.bfloat16)
        term = lax.dot_general(window, wbuf[tap], COLS_T, preferred_element_type=jnp.float32)
        acc = term if acc is None else acc + term
    out_ref[0] = acc.astype(jnp.bfloat16)

    cq.wait_recv()
    cq2.wait_recv()
    scale = 1.0 / math.sqrt(NZ * NY * NC * 2 * 2 * slots)
    pair_ref[...] = final[...].astype(jnp.float32) * scale
    for hop in [None] + hops:
        def sent(hop=hop):
            y_copy(hop).wait_send()
            x_copy_w(hop).wait_send()
            for kind in range(3):
                core_copy(kind, hop).wait_send()
        when(hop, sent)
    for d in range(2):
        for s in range(NZ - 1):
            leaves = (z < NZ - 1) & (z >= s) if d == 0 else (z > 0) & (z + s < NZ)
            @pl.when(leaves)
            def _(d=d, s=s):
                z_copy(d, s).wait_send()
    for cp in [trunk_copy, d_copy, t_copy, h_copy, c_copy, c_copy2, x_copy, cq, cq2] + ag + xf:
        cp.wait_send()


def per_device_kernel(pre_act, trunk_grad, conv_weight, pair_weight, donor_slots, accept_slots, junction_grad, pair_counts):
    slab, chan = pre_act.shape[1:]
    slots = donor_slots.shape[3]
    hc = chan // 2
    bf, f32 = jnp.bfloat16, jnp.float32
    V = pltpu.VMEM
    D = pltpu.SemaphoreType.DMA
    scratch = [
        V(pre_act.shape, bf), V(pair_weight.shape, bf), V(donor_slots.shape, jnp.int32),
        V(accept_slots.shape, jnp.int32), V(junction_grad.shape, f32), V(pair_counts.shape, jnp.int32),
        V((slab // 2, hc), bf), D((8,)),
        V((slab, chan), bf), V((slab, chan), f32), V((conv_weight.shape[0], chan, chan), bf),
        V((slab // 2, hc), bf), V((slots, chan), bf), V((slots, chan), bf),
        V((slots, chan), bf), V((slots, chan), bf), V((2 * slots, chan), bf),
        V((2 * slots, chan), bf), V((4 * slots + slab // 2, chan), bf),
        V((slab + 16, chan), f32), V((8, chan), f32), V((8, chan), f32),
        V((chan, chan), f32), V((2, hc, hc), bf), V((2, hc, hc), bf), V((hc, hc), bf), V((hc, hc), bf),
        V((hc, hc), f32), V((hc, hc), bf), V((7, hc // 8, hc), bf), V((chan, chan), bf),
        D((6,)), D((6,)), D((7,)), D((7,)), D((7,)), D((7,)), D((21,)), D((21,)), D((4,)), D((4,)),
        D((6,)), D((6,)), D((7,)), D((7,)), D((7,)), D((7,)), D((8,)), D((8,)),
    ]
    return pl.pallas_call(
        kernel,
        out_shape=(jax.ShapeDtypeStruct(pre_act.shape, bf), jax.ShapeDtypeStruct((chan, chan), f32)),
        in_specs=[pl.BlockSpec(memory_space=pltpu.HBM)] * 8,
        out_specs=[pl.BlockSpec(memory_space=pltpu.VMEM)] * 2,
        scratch_shapes=scratch,
        compiler_params=pltpu.CompilerParams(
            collective_id=0, has_side_effects=True, vmem_limit_bytes=40 << 20),
    )(*[
        pltpu.with_memory_space_constraint(a, pltpu.HBM)
        for a in (pre_act, trunk_grad, conv_weight, pair_weight, donor_slots, accept_slots,
                  junction_grad, pair_counts)
    ])


def solution(mesh):
    in_specs = (
        P("dp", "seq", None),
        P("dp", None, "seq"),
        P(None, "dp", None),
        P(),
        P("dp", "seq", None, None),
        P("dp", "seq", None, None),
        P("dp", "seq", None, None),
        P("dp", None, None),
    )
    out_specs = (P("dp", "seq", None), P())
    fits = mesh.shape["dp"] == NZ * NY * NC and mesh.shape["seq"] == 2
    return jax.shard_map(
        per_device_kernel if fits else per_device_general, mesh=mesh, in_specs=in_specs, out_specs=out_specs, check_vma=False
    )
```
